32 devices in a mesh: dp: 16 (over z, x, core), tp: 2 (over y).
Axes of the slice: x: 2, y: 2, z: 4, core: 2. Of those that a mesh axis runs over, the one named last changes fastest.
Arguments:
- q_nope: bfloat16 [512, 2048], P('dp', 'tp'), may hold values from -4 to 4
- q_rope: bfloat16 [512, 1024], P('dp', 'tp'), may hold values from -80 to 80
- lengths: int32 [512], P('dp'), may hold values from 1 to 512, as said below
- page_table: int32 [512, 8], P('dp'), may hold values from 0 to 95, as said below
- lend_counts: int32 [512, 2], P('dp'), may hold values from 0 to 2, as said below
- latent_pages: bfloat16 [1536, 64, 512], P('dp'), may hold values from -5 to 5
- rope_pages: bfloat16 [1536, 4096], P('dp'), may hold values from -4 to 4
- w_uk: bfloat16 [16, 128, 512], P('tp'), may hold values from -0.5 to 0.5
- w_uv: bfloat16 [16, 512, 128], P('tp'), may hold values from -0.75 to 0.75
- w_o: bfloat16 [2048, 2048], P('tp'), may hold values from -0.125 to 0.125
Outputs:
- attention_out: bfloat16 [512, 2048], P('dp', 'tp')
The draws below stay inside these ranges and needn't reach their ends.
Inputs may be any that keep to these rules, and one draw needn't show every extreme that they name: `lengths`: at least one live token in every request; some request reaches the most in every draw. For every request lend_counts[r, 0] + lend_counts[r, 1] is below its page count, so its first page is held by its own replica; every replica has a request that lends 2 pages each way. `page_table`: the 8 entries of a row are distinct. Entries for pages past a request's page count are not read.
All inputs are finite; a program needn't handle non-finite values.
Results may differ from the reference program's by a relative error of at most 0.012.
Values may be sent and summed in bfloat16 or wider, within the bound.
No kernel may reach another device: no remote copies, remote signals or barrier semaphores. Data moves between devices by JAX's collectives and lax.ppermute only.
A program may use at most 128 MiB of HBM per device.

```python
import math
import jax
import jax.numpy as jnp
from jax import lax

D = 2048
HEADS = 16
LATENT = 512
ROPE = 64
NOPE = 128
VDIM = 128
PAGE = 64
MAXP = 8
LEND = 2
REQS = 32
PAGES_DEV = 96
REQS_ALL = 512
PAGES_ALL = 1536
N_DP = 16


def lend_plan(key):
    base_key = jax.random.fold_in(key, 11)
    key_busy, key_long, key_short, key_chosen, key_left, key_right, key_lender, key_full = jax.random.split(base_key, 8)
    replicas = REQS_ALL // REQS
    busy_replica = jax.random.randint(key_busy, (replicas,), 0, 4) == 0
    busy_rows = jnp.repeat(busy_replica, REQS)
    top_len = MAXP * PAGE
    long_len = jax.random.randint(key_long, (REQS_ALL,), top_len // 2, top_len + 1)
    short_len = jax.random.randint(key_short, (REQS_ALL,), 1, top_len // 4 + 1)
    req_lens = jnp.where(busy_rows, long_len, short_len)
    row_ids = jnp.arange(REQS_ALL, dtype=jnp.int32)
    lender_slot = jax.random.randint(key_lender, (replicas,), 0, REQS)
    lender_rows = jnp.arange(replicas, dtype=jnp.int32) * REQS + lender_slot
    is_lender = jnp.any(row_ids[:, None] == lender_rows[None, :], axis=1)
    full_len = jax.random.randint(key_full, (REQS_ALL,), (MAXP - 1) * PAGE + 1, top_len + 1)
    req_lens = jnp.where(is_lender, full_len, req_lens)
    chosen = jax.random.randint(key_chosen, (), 0, REQS_ALL)
    req_lens = jnp.where(row_ids == chosen, top_len, req_lens)
    page_count = (req_lens + PAGE - 1) // PAGE
    lend_left = jnp.minimum(jax.random.randint(key_left, (REQS_ALL,), 0, LEND + 1), (page_count - 1) // 2)
    lend_right = jnp.minimum(jax.random.randint(key_right, (REQS_ALL,), 0, LEND + 1), page_count - 1 - lend_left)
    forced = is_lender | (row_ids == chosen)
    lend_left = jnp.where(forced, LEND, lend_left)
    lend_right = jnp.where(forced, LEND, lend_right)
    return (req_lens.astype(jnp.int32), jnp.stack([lend_left, lend_right], axis=1).astype(jnp.int32))


def draw_lengths(key, part):
    return lend_plan(key)[0]


def draw_lend_counts(key, part):
    return lend_plan(key)[1]


def draw_page_table(key, part):
    row_keys = jax.random.split(jax.random.fold_in(key, 41), REQS_ALL)
    picked = jax.vmap(lambda one: jax.random.permutation(one, PAGES_DEV)[:MAXP])(row_keys)
    return picked.astype(jnp.int32)


def draw_q_rope(key, part):
    key_noise = jax.random.fold_in(jax.random.fold_in(key, 23), 0)
    values = jax.random.truncated_normal(key_noise, -4.0, 4.0, (REQS_ALL, HEADS, ROPE), jnp.float32)
    return values.reshape(REQS_ALL, HEADS * ROPE).astype(jnp.bfloat16)


def draw_rope_pages(key, part):
    key_noise = jax.random.fold_in(jax.random.fold_in(key, 31), 0)
    values = jax.random.truncated_normal(key_noise, -4.0, 4.0, (PAGES_ALL, PAGE, ROPE), jnp.float32)
    return values.reshape(PAGES_ALL, PAGE * ROPE).astype(jnp.bfloat16)


def steps_of(stream_key, extent, pieces, smallest, largest):
    factor_of, own = 1.0, jax.random.fold_in(stream_key, 6)
    for dim, blocks in pieces:
        steps = jnp.exp(jax.random.uniform(jax.random.fold_in(own, dim), (blocks,), jnp.float32, smallest / len(pieces), largest / len(pieces)))
        factor_of = factor_of * jnp.repeat(steps, extent[dim] // blocks).reshape([-1 if axis == dim else 1 for axis in range(len(extent))])
    return factor_of


def scatter_about(stream_key, shape, width, limit, pieces=(), kind=jnp.bfloat16):
    gain = steps_of(stream_key, shape, pieces, -0.22, 0.18) if pieces else 1.0
    array = jax.random.normal(stream_key, shape, jnp.float32) * width * gain
    return jnp.minimum(jnp.maximum(array, -limit), limit).astype(kind)


def setup_inputs(seed: int = 0) -> dict:
    splits = jax.random.split(jax.random.key(seed), 11)
    return {
        "q_nope": scatter_about(splits[0], (REQS_ALL, HEADS * NOPE), 1.0, 4.0, ((0, 16), (1, 2))),
        "q_rope": draw_q_rope(jax.random.fold_in(splits[10], 71), 0),
        "lengths": draw_lengths(jax.random.fold_in(splits[10], 71), 0),
        "page_table": draw_page_table(jax.random.fold_in(splits[10], 71), 0),
        "lend_counts": draw_lend_counts(jax.random.fold_in(splits[10], 71), 0),
        "latent_pages": scatter_about(splits[5], (PAGES_ALL, PAGE, LATENT), 1.0, 5.0, ((0, 16),)),
        "rope_pages": draw_rope_pages(jax.random.fold_in(splits[10], 71), 0),
        "w_uk": scatter_about(splits[7], (HEADS, NOPE, LATENT), NOPE ** -0.5, 0.5, ((0, 2),)),
        "w_uv": scatter_about(splits[8], (HEADS, LATENT, VDIM), (LATENT // 8) ** -0.5, 0.75, ((0, 2),)),
        "w_o": scatter_about(splits[9], (HEADS * VDIM, D), (HEADS * VDIM) ** -0.5, 0.125, ((0, 2),)),
    }


def reference(q_nope, q_rope, lengths, page_table, lend_counts, latent_pages, rope_pages, w_uk, w_uv, w_o):
    score_scale = 1.0 / math.sqrt(NOPE + ROPE)
    query_lat = jnp.einsum('rhn,hnc->rhc', q_nope.reshape(REQS_ALL, HEADS, NOPE).astype(jnp.float32), w_uk.astype(jnp.float32)).astype(jnp.bfloat16)
    query_rope = q_rope.reshape(REQS_ALL, HEADS, ROPE)
    rope_table = rope_pages.reshape(PAGES_ALL, PAGE, ROPE)

    def replica(index):
        row_start = (index * REQS).astype(jnp.int32)
        req_lens = lax.dynamic_slice_in_dim(lengths, row_start, REQS)
        slot_table = lax.dynamic_slice_in_dim(page_table, row_start, REQS)
        lend_rows = lax.dynamic_slice_in_dim(lend_counts, row_start, REQS)
        own_query = lax.dynamic_slice_in_dim(query_lat, row_start, REQS)
        own_rope = lax.dynamic_slice_in_dim(query_rope, row_start, REQS)
        page_count = (req_lens + PAGE - 1) // PAGE
        first_lent = (page_count - lend_rows[:, 0] - lend_rows[:, 1])[:, None]
        second = (page_count - lend_rows[:, 1])[:, None]
        page_ids = jnp.arange(MAXP, dtype=jnp.int32)[None, :]
        holder_step = jnp.where(page_ids < first_lent, 0, jnp.where(page_ids < second, N_DP - 1, 1)).astype(jnp.int32)
        holder = (index + holder_step) % N_DP
        pool_rows = (holder * PAGES_DEV + slot_table).astype(jnp.int32)
        latent = latent_pages[pool_rows].reshape(REQS, MAXP * PAGE, LATENT).astype(jnp.float32)
        rope_keys = rope_table[pool_rows].reshape(REQS, MAXP * PAGE, ROPE).astype(jnp.float32)
        positions = jnp.arange(MAXP * PAGE, dtype=jnp.int32)[None, :]
        alive_mask = positions < req_lens[:, None]
        scores = (jnp.einsum('rhc,rtc->rht', own_query.astype(jnp.float32), latent) + jnp.einsum('rhe,rte->rht', own_rope.astype(jnp.float32), rope_keys)) * score_scale
        scores = jnp.where(alive_mask[:, None, :], scores, -jnp.inf)
        peak = lax.optimization_barrier(jnp.max(scores, axis=-1, keepdims=True))
        weights = jnp.exp(scores - peak).astype(jnp.bfloat16).astype(jnp.float32)
        total = lax.optimization_barrier(jnp.sum(weights, axis=-1))
        context = jnp.einsum('rht,rtc->rhc', weights, latent) / total[..., None]
        return context.astype(jnp.bfloat16)
    contexts = lax.map(replica, jnp.arange(N_DP, dtype=jnp.int32)).reshape(REQS_ALL, HEADS, LATENT)
    head_outs = jnp.einsum('rhc,hcv->rhv', contexts.astype(jnp.float32), w_uv.astype(jnp.float32)).astype(jnp.bfloat16)
    head_outs = head_outs.reshape(REQS_ALL, HEADS * VDIM)
    return jnp.dot(head_outs, w_o, preferred_element_type=jnp.float32).astype(jnp.bfloat16)
```

```python
import functools
import math

import jax
import jax.numpy as jnp
from jax import lax
from jax.experimental import pallas as pl
from jax.experimental.pallas import tpu as pltpu
from jax.sharding import PartitionSpec as P

LEND = 2
LANES = 128
FIELDS = 16
FAR = -1e30
UNROLL = 8
MIB = 1 << 20


def swap(block, axis, odd_first):
    count = lax.axis_size(axis)
    shift = 1 if odd_first else 0
    pairs = []
    for start in range(shift, count + shift, 2):
        a, b = start % count, (start + 1) % count
        pairs += [(a, b), (b, a)]
    return lax.ppermute(block, axis, pairs)


def lane_tile(ref, index):
    return ref[:, index * LANES : (index + 1) * LANES]


def pack_kernel(lengths, table, lend, q_nope, q_rope, message, own, *, page):
    rows = q_nope.shape[0]
    most = table.shape[0]
    shift = page.bit_length() - 1
    wide, narrow = q_nope.shape[1], q_rope.shape[1]
    message[:, :wide] = q_nope[...]
    message[:, wide : wide + narrow] = q_rope[...]
    length = lengths[...]
    count = lax.shift_right_logical(length + (page - 1), shift)
    to_prev, to_next = lend[0:1, :], lend[1:2, :]
    held = count - to_prev - to_next

    def pick(index):
        found = jnp.zeros_like(index)
        for k in range(most):
            found = jnp.where(index == k, table[k : k + 1, :], found)
        return found

    def lent(first, number):
        slots = [pick(jnp.minimum(first + k, count - 1)) for k in range(LEND)]
        live = jnp.minimum(length - first * page, number * page)
        return [*slots, jnp.maximum(live, 0)]

    def stack(fields):
        row = lax.broadcasted_iota(jnp.int32, (FIELDS, rows), 0)
        block = jnp.zeros((FIELDS, rows), jnp.int32)
        for k, field in enumerate(fields):
            block = jnp.where(row == k, jnp.broadcast_to(field, (FIELDS, rows)), block)
        return block

    prev, nxt = lent(held, to_prev), lent(count - to_next, to_next)
    odd = lax.rem(lax.axis_index("dp"), 2) == 1
    first = [jnp.where(odd, p, n) for p, n in zip(prev, nxt)]
    second = [jnp.where(odd, n, p) for p, n in zip(prev, nxt)]
    message[:, wide + narrow :] = jnp.zeros((rows, LANES), message.dtype)
    message[0:FIELDS, wide + narrow : wide + narrow + rows] = (
        stack([*first, *second]).astype(jnp.float32).astype(message.dtype)
    )
    own[...] = jnp.zeros_like(own)
    mine = [pick(jnp.minimum(k, held - 1)) for k in range(most)]
    own[:, :rows] = stack([*mine, jnp.minimum(length, held * page)])


def project_queries(message, w_uk, queries, heads, latent, narrow):
    rows = message.shape[0]
    nope = w_uk.shape[1]
    tiles = latent // LANES
    low = lax.broadcasted_iota(jnp.int32, (rows, LANES), 1) < LANES // 2
    for h in range(heads):
        lat = jnp.dot(
            message[:, h * nope : (h + 1) * nope], w_uk[h], preferred_element_type=jnp.float32
        )
        for c in range(tiles):
            queries[c, pl.ds(h, rows, stride=heads), :] = lat[:, c * LANES : (c + 1) * LANES]
    for c in range(narrow // LANES):
        pair = lane_tile(message, heads * nope // LANES + c).astype(jnp.float32)
        swapped = pltpu.roll(pair, LANES // 2, 1)
        for h, left, right in ((2 * c, pair, swapped), (2 * c + 1, swapped, pair)):
            at = pl.ds(h, rows, stride=heads)
            queries[tiles, at, :] = jnp.where(low, left, 0.0)
            queries[tiles + 1, at, :] = jnp.where(low, 0.0, right)


def list_work(plan, work, live_row, rows, units, tokens):
    shift = tokens.bit_length() - 1
    found = 0
    for r in range(rows):
        for j in range(units):
            work[found + j] = LEND * j * LANES + r
        found = found + lax.shift_right_logical(plan[live_row, r] + (tokens - 1), shift)
    for u in range(UNROLL):
        work[found + u] = rows
    return lax.div(found + (UNROLL - 1), UNROLL)


def split_code(code):
    return code & (LANES - 1), lax.shift_right_logical(code, LANES.bit_length() - 1)


def rope_lanes(page, heads):
    quarter = page // 4
    lane = lax.broadcasted_iota(jnp.int32, (heads, LEND * page), 1)
    return lane // page * quarter + lax.rem(lane, page) // 4, lax.rem(lane, 4)


def score(queries, pool, rope_keys, r, slots, lanes, heads):
    start = pl.multiple_of(r * heads, heads)
    tiles = queries.shape[0] - 2
    query = jnp.concatenate([queries[c, pl.ds(start, heads), :] for c in range(tiles)], axis=1)
    keys = jnp.concatenate([pool[s] for s in slots], axis=0)
    both = (((1,), (1,)), ((), ()))
    found = lax.dot_general(
        query.astype(jnp.bfloat16), keys, both, preferred_element_type=jnp.float32
    )
    turned = jnp.concatenate(
        [queries[tiles, pl.ds(start, heads), :], queries[tiles + 1, pl.ds(start, heads), :]], axis=0
    ).astype(jnp.bfloat16)
    none = jnp.zeros_like(turned)
    four = jnp.concatenate(
        [
            jnp.concatenate([turned, none], axis=1),
            jnp.concatenate([none, turned], axis=1),
        ],
        axis=0,
    )
    rope = jnp.concatenate([rope_keys[s] for s in slots], axis=0)
    columns = rope.shape[0]
    rope = jnp.concatenate(
        [rope, jnp.zeros((found.shape[1] - columns, rope.shape[1]), rope.dtype)], axis=0
    )
    parts = lax.dot_general(four, rope, both, preferred_element_type=jnp.float32)
    source, which = lanes
    for j in range(4):
        moved = jnp.take_along_axis(parts[j * heads : (j + 1) * heads, :], source, axis=1)
        extra = moved if j == 0 else jnp.where(which == j, moved, extra)
    return found + extra


def score_work(queries, pool, rope_keys, scores, plan, work, blocks, base, live_row, heads, scale):
    page = pool.shape[1]
    tokens = LEND * page
    scores[...] = jnp.full_like(scores, FAR)
    position = lax.broadcasted_iota(jnp.int32, (heads, tokens), 1)
    lanes = rope_lanes(page, heads)

    @pl.loop(0, blocks)
    def _(block):
        for u in range(UNROLL):
            r, first = split_code(work[block * UNROLL + u])
            j = lax.shift_right_logical(first, 1)
            ids = [plan[base + first + k, r] for k in range(LEND)]
            found = score(queries, pool, rope_keys, r, ids, lanes, heads) * scale
            start = pl.multiple_of(r * heads, heads)
            scores[j, pl.ds(start, heads), :] = jnp.where(
                position < plan[live_row, r] - j * tokens, found, FAR
            )


def soften(scores, weights, norm, lse, total_rows):
    units = scores.shape[0]
    step = 64
    for r in range(0, total_rows, step):
        block = [scores[j, r : r + step, :] for j in range(units)]
        top = block[0]
        for one in block[1:]:
            top = jnp.maximum(top, one)
        peak = jnp.max(top, axis=-1, keepdims=True)
        total = jnp.zeros((step, LANES), jnp.float32)
        for j in range(units):
            rounded = jnp.exp(block[j] - peak).astype(jnp.bfloat16)
            weights[j, r : r + step, :] = rounded
            total = total + rounded.astype(jnp.float32)
        total = jnp.sum(total, axis=-1, keepdims=True)
        norm[r : r + step, :] = jnp.broadcast_to(1.0 / total, (step, LANES))
        lse[r : r + step, :] = jnp.broadcast_to(peak + jnp.log(total), (step, LANES))


def value_work(pool, weights, context, plan, work, blocks, base, heads, add):
    context[...] = jnp.zeros_like(context)

    @pl.loop(0, blocks)
    def _(block):
        for u in range(UNROLL):
            r, first = split_code(work[block * UNROLL + u])
            j = lax.shift_right_logical(first, 1)
            start = pl.multiple_of(r * heads, heads)
            values = jnp.concatenate([pool[plan[base + first + k, r]] for k in range(LEND)], axis=0)
            summed = jnp.dot(
                weights[j, pl.ds(start, heads), :], values, preferred_element_type=jnp.float32
            )
            for c in range(context.shape[0]):
                part = summed[:, c * LANES : (c + 1) * LANES]
                if add:
                    part = part + context[c, pl.ds(start, heads), :]
                context[c, pl.ds(start, heads), :] = part


def head_out(context, norm, w_uv, h, rows, heads):
    at = pl.ds(h, rows, stride=heads)
    scale = norm[at, :]
    ctx = jnp.concatenate([context[c, at, :] * scale for c in range(context.shape[0])], axis=1)
    return jnp.dot(ctx.astype(jnp.bfloat16), w_uv[h], preferred_element_type=jnp.float32)


def own_scores_kernel(
    own, message, rope_hbm, pool_hbm, w_uk_hbm,
    pool, rope_keys, weights, norm, lse,
    queries, scores, spread, rope_pages, w_uk, plan, work, sems,
    *, heads, narrow,
):
    slots, page, latent = pool.shape
    rows = message.shape[0]
    units = weights.shape[0]
    scale = 1.0 / math.sqrt(w_uk.shape[1] + narrow // heads)
    routes = (
        (rope_hbm, rope_pages),
        (own, plan),
        (w_uk_hbm, w_uk),
        (pool_hbm, pool),
    )
    fetches = [pltpu.make_async_copy(*route, sems.at[k]) for k, route in enumerate(routes)]
    for fetch in fetches:
        fetch.start()
    fetches[0].wait()
    pieces = page // 2
    pitch = pieces + 1
    for c in range(pieces):
        spread[pl.ds(c, slots, stride=pitch), :] = lane_tile(rope_pages, c).astype(jnp.float32)
    for s in range(slots):
        for side in range(2):
            rows_of = spread[pl.ds(s * pitch + side, pieces // 2, stride=2), :]
            rope_keys[s, :, side * LANES : (side + 1) * LANES] = rows_of.astype(jnp.bfloat16)
    fetches[1].wait()
    blocks = list_work(plan, work, LEND * units, rows, units, LEND * page)
    fetches[2].wait()
    project_queries(message, w_uk, queries, heads, latent, narrow)
    fetches[3].wait()
    score_work(
        queries, pool, rope_keys, scores, plan, work, blocks, 0, LEND * units, heads, scale
    )
    soften(scores, weights, norm, lse, rows * heads)


def own_values_kernel(own, pool, weights, norm, w_uv, outs, context, plan, work, plan_sem, *, heads):
    page = pool.shape[1]
    rows = outs.shape[0]
    units = weights.shape[0]
    fetch_plan = pltpu.make_async_copy(own, plan, plan_sem)
    fetch_plan.start()
    fetch_plan.wait()
    blocks = list_work(plan, work, LEND * units, rows, units, LEND * page)
    value_work(pool, weights, context, plan, work, blocks, 0, heads, True)
    width = w_uv.shape[2]
    for h in range(heads):
        outs[:, h * width : (h + 1) * width] = head_out(context, norm, w_uv, h, rows, heads)


def serve_kernel(
    message, pool, rope_keys, w_uk, w_uv, back,
    queries, scores, weights, norm, lse, context, fields, plan, work, plan_sem,
    *, narrow, base,
):
    rows = message.shape[0]
    slots, page, latent = pool.shape
    heads = w_uk.shape[0]
    scale = 1.0 / math.sqrt(w_uk.shape[1] + narrow // heads)
    asked = message[0:FIELDS, message.shape[1] - LANES :]
    fields[...] = asked.astype(jnp.float32).astype(jnp.int32)
    fetch_plan = pltpu.make_async_copy(fields, plan, plan_sem)
    fetch_plan.start()
    project_queries(message, w_uk, queries, heads, latent, narrow)
    fetch_plan.wait()
    blocks = list_work(plan, work, base + LEND, rows, 1, LEND * page)
    score_work(
        queries, pool, rope_keys, scores, plan, work, blocks, base, base + LEND, heads, scale
    )
    soften(scores, weights, norm, lse, rows * heads)
    value_work(pool, weights, context, plan, work, blocks, base, heads, False)
    width = w_uv.shape[2]
    lane = lax.broadcasted_iota(jnp.int32, (rows, LANES), 1)
    logs = jnp.zeros((rows, LANES), jnp.float32)
    for h in range(heads):
        back[:, h * width : (h + 1) * width] = head_out(
            context, norm, w_uv, h, rows, heads
        ).astype(jnp.bfloat16)
        logs = jnp.where(lax.rem(lane, heads) == h, lse[pl.ds(h, rows, stride=heads), :], logs)
    packed = jnp.zeros((rows, LANES), jnp.float32)
    for part in range(3):
        piece = logs.astype(jnp.bfloat16).astype(jnp.float32)
        logs = logs - piece
        packed = jnp.where(lane // heads == part, piece, packed)
    back[:, heads * width :] = packed.astype(jnp.bfloat16)


def join_kernel(outs, lse, from_a, from_b, w_o, sent, kept, joined, *, heads):
    rows = outs.shape[0]
    width = outs.shape[1] // heads
    totals = []
    for arrived in (from_a, from_b):
        tile = arrived[:, heads * width :].astype(jnp.float32)
        total = tile + pltpu.roll(tile, LANES - heads, 1) + pltpu.roll(tile, LANES - 2 * heads, 1)
        totals.append(total)
    for h in range(heads):
        at = slice(h * width, (h + 1) * width)
        logs = [lse[pl.ds(h, rows, stride=heads), :]]
        values = [outs[:, at]]
        for arrived, total in zip((from_a, from_b), totals):
            logs.append(jnp.broadcast_to(total[:, h : h + 1], (rows, LANES)))
            values.append(arrived[:, at].astype(jnp.float32))
        peak = jnp.maximum(jnp.maximum(logs[0], logs[1]), logs[2])
        shares = [jnp.exp(one - peak) for one in logs]
        top = shares[0] * values[0] + shares[1] * values[1] + shares[2] * values[2]
        joined[:, at] = (top / (shares[0] + shares[1] + shares[2])).astype(jnp.bfloat16)
    mine = lax.axis_index("tp")
    other = lax.rem(mine + 1, lax.axis_size("tp"))
    cols = sent.shape[1]
    heads_joined = joined[...]
    away = pl.ds(pl.multiple_of(other * cols, cols), cols)
    here = pl.ds(pl.multiple_of(mine * cols, cols), cols)
    sent[...] = jnp.dot(
        heads_joined, w_o[:, away], preferred_element_type=jnp.float32
    ).astype(jnp.bfloat16)
    kept[...] = jnp.dot(heads_joined, w_o[:, here], preferred_element_type=jnp.float32)


def vmem():
    return pl.BlockSpec(memory_space=pltpu.VMEM)


def in_hbm(array):
    return pltpu.with_memory_space_constraint(array, pltpu.HBM)


def call(kernel, name, out, ins, scratch, limit, cost=None, **sizes):
    return pl.pallas_call(
        functools.partial(kernel, **sizes),
        name=name,
        out_shape=out,
        in_specs=ins,
        out_specs=jax.tree.map(lambda _: vmem(), out),
        scratch_shapes=scratch,
        compiler_params=pltpu.CompilerParams(vmem_limit_bytes=limit * MIB),
        cost_estimate=cost,
    )


def shards(
    q_nope, q_rope, lengths, page_table, lend_counts, latent_pages, rope_pages, w_uk, w_uv, w_o
):
    rows = lengths.shape[0]
    heads, nope, latent = w_uk.shape
    slots, page, _ = latent_pages.shape
    most = page_table.shape[1]
    width = w_uv.shape[2]
    narrow = q_rope.shape[1]
    tiles = latent // LANES
    units = most // LEND
    f32, bf16, i32 = jnp.float32, jnp.bfloat16, jnp.int32
    shape = jax.ShapeDtypeStruct
    sem = pltpu.SemaphoreType.DMA
    stats = (rows * heads, LANES)
    padded = (rows + 1) * heads
    block = pltpu.VMEM((tiles + 2, padded, LANES), f32)
    contexts = pltpu.VMEM((tiles, padded, LANES), f32)
    plan = pltpu.SMEM((FIELDS, LANES), i32)
    work = pltpu.SMEM((rows * units + UNROLL,), i32)

    message, own = call(
        pack_kernel,
        "pack",
        (shape((rows, heads * nope + narrow + LANES), bf16), shape((FIELDS, LANES), i32)),
        [vmem()] * 5,
        [],
        4,
        page=page,
    )(*map(in_hbm, (lengths.reshape(1, rows), page_table.T, lend_counts.T, q_nope, q_rope)))
    asked_a = swap(message, "dp", False)
    asked_b = swap(message, "dp", True)

    pool, rope_keys, weights, norm, lse = call(
        own_scores_kernel,
        "own_scores",
        (
            shape((slots, page, latent), bf16),
            shape((slots, page // 4, 2 * LANES), bf16),
            shape((units, padded, LANES), bf16),
            shape(stats, f32),
            shape(stats, f32),
        ),
        [vmem()] * 2 + [pl.BlockSpec(memory_space=pl.ANY)] * 3,
        [
            block,
            pltpu.VMEM((units, padded, LANES), f32),
            pltpu.VMEM((slots * (page // 2 + 1), LANES), f32),
            pltpu.VMEM(rope_pages.shape, bf16),
            pltpu.VMEM(w_uk.shape, bf16),
            plan,
            work,
            sem((4,)),
        ],
        24,
        pl.CostEstimate(
            flops=2 * rows * heads * most * page * (latent + LANES),
            bytes_accessed=slots * page * (latent + LANES) * 2,
            transcendentals=rows * heads * most * page,
        ),
        heads=heads,
        narrow=narrow,
    )(own, message, *map(in_hbm, (rope_pages, latent_pages, w_uk)))

    serve_scratch = [
        block,
        pltpu.VMEM((1, padded, LANES), f32),
        pltpu.VMEM((1, padded, LANES), bf16),
        pltpu.VMEM(stats, f32),
        pltpu.VMEM(stats, f32),
        contexts,
        pltpu.VMEM((FIELDS, LANES), i32),
        plan,
        work,
        sem(()),
    ]

    def serve(asked, name, base):
        return call(
            serve_kernel,
            name,
            shape((rows, heads * width + LANES), bf16),
            [vmem()] * 5,
            serve_scratch,
            8,
            narrow=narrow,
            base=base,
        )(asked, pool, rope_keys, w_uk, w_uv)

    from_b = swap(serve(asked_b, "serve_b", LEND + 1), "dp", True)
    from_a = swap(serve(asked_a, "serve_a", 0), "dp", False)
    outs = call(
        own_values_kernel,
        "own_values",
        shape((rows, heads * width), f32),
        [vmem()] * 5,
        [contexts, plan, work, sem(())],
        8,
        heads=heads,
    )(own, pool, weights, norm, w_uv)
    cols = w_o.shape[1] // lax.axis_size("tp")
    sent, kept = call(
        join_kernel,
        "join",
        (shape((rows, cols), bf16), shape((rows, cols), f32)),
        [vmem()] * 5,
        [pltpu.VMEM((rows, heads * width), bf16)],
        8,
        heads=heads,
    )(outs, lse, from_a, from_b, w_o)
    return (kept + swap(sent, "tp", False).astype(f32)).astype(bf16)


def solution(mesh):
    in_specs = (
        P("dp", "tp"),
        P("dp", "tp"),
        P("dp"),
        P("dp", None),
        P("dp", None),
        P("dp", None, None),
        P("dp", None),
        P("tp", None, None),
        P("tp", None, None),
        P("tp", None),
    )
    out_specs = P("dp", "tp")
    return jax.shard_map(shards, mesh=mesh, in_specs=in_specs, out_specs=out_specs, check_vma=False)
```

```python
import functools
import math

import jax
import jax.numpy as jnp
from jax import lax
from jax.experimental import pallas as pl
from jax.experimental.pallas import tpu as pltpu
from jax.sharding import PartitionSpec as P

LEND = 2
LANES = 128
FIELDS = 16
ROW, LIVE, COUNT, SCORE_ROW = 2, 3, 4, 5
TABLE_ROWS = 6
FAR = -1e30
UNROLL = 8
PAIR = 2
MIB = 1 << 20


def swap(block, axis, odd_first):
    count = lax.axis_size(axis)
    shift = 1 if odd_first else 0
    pairs = []
    for start in range(shift, count + shift, 2):
        a, b = start % count, (start + 1) % count
        pairs += [(a, b), (b, a)]
    return lax.ppermute(block, axis, pairs)


def lane_tile(ref, index):
    return ref[:, index * LANES : (index + 1) * LANES]


def compact(fields, live_row, segment, spacing):
    height, lanes = fields.shape
    row = lax.broadcasted_iota(jnp.int32, (lanes, lanes), 0)
    column = lax.broadcasted_iota(jnp.int32, (lanes, lanes), 1)
    kept = jnp.where(fields[live_row : live_row + 1, :] > 0.0, 1.0, 0.0)
    kept = jnp.broadcast_to(kept, (height, lanes))
    ahead = (row // segment == column // segment) & (row < column)
    inside = row // segment == column // spacing
    place = jnp.dot(
        kept.astype(jnp.bfloat16),
        jnp.where(ahead, 1.0, 0.0).astype(jnp.bfloat16),
        preferred_element_type=jnp.float32,
    )
    count = jnp.dot(
        kept.astype(jnp.bfloat16),
        jnp.where(inside, 1.0, 0.0).astype(jnp.bfloat16),
        preferred_element_type=jnp.float32,
    )
    lane = lax.broadcasted_iota(jnp.int32, (height, lanes), 1)
    target = place.astype(jnp.int32) + lane // segment * spacing
    target = jnp.where(kept > 0.0, target, -1)
    chosen = jnp.where(jnp.broadcast_to(target[0:1, :], (lanes, lanes)) == row, 1.0, 0.0)
    moved = lax.dot_general(
        fields.astype(jnp.bfloat16),
        chosen.astype(jnp.bfloat16),
        (((1,), (1,)), ((), ())),
        preferred_element_type=jnp.float32,
    )
    return moved, count


def pack_kernel(lengths, table, lend, q_nope, q_rope, message, own, fields, *, page):
    rows = q_nope.shape[0]
    most = table.shape[0]
    shift = page.bit_length() - 1
    wide, narrow = q_nope.shape[1], q_rope.shape[1]
    length = lengths[...]
    count = lax.shift_right_logical(length + (page - 1), shift)
    to_prev, to_next = lend[0:1, :], lend[1:2, :]
    held = count - to_prev - to_next
    request = lax.broadcasted_iota(jnp.int32, (1, rows), 1)

    def pick(index):
        found = jnp.zeros_like(index)
        for k in range(most):
            found = jnp.where(index == k, table[k : k + 1, :], found)
        return found

    def lent(first, number):
        slots = [pick(jnp.minimum(first + k, count - 1)) for k in range(LEND)]
        live = jnp.minimum(length - first * page, number * page)
        return [*slots, request + 1, jnp.maximum(live, 0)]

    def stack(values, height):
        row = lax.broadcasted_iota(jnp.int32, (height, rows), 0)
        block = jnp.zeros((height, rows), jnp.int32)
        for k, value in enumerate(values):
            block = jnp.where(row == k, jnp.broadcast_to(value, (height, rows)), block)
        return block

    prev, nxt = lent(held, to_prev), lent(count - to_next, to_next)
    odd = lax.rem(lax.axis_index("dp"), 2) == 1
    fields[...] = jnp.zeros_like(fields)
    for k, (yes, no) in enumerate(((prev, nxt), (nxt, prev))):
        mine = stack([jnp.where(odd, p, n) for p, n in zip(yes, no)], FIELDS)
        fields[:, k * rows : (k + 1) * rows] = mine.astype(jnp.float32)
    moved, counts = compact(fields[...], LIVE, rows, LANES // 2)
    row = lax.broadcasted_iota(jnp.int32, (FIELDS, LANES), 0)
    asked = jnp.where(row == COUNT, counts, moved).astype(message.dtype)
    message[:, :wide] = q_nope[...]
    message[:, wide : wide + narrow] = q_rope[...]
    message[:, wide + narrow :] = jnp.concatenate(
        [asked, jnp.zeros((rows - FIELDS, LANES), message.dtype)], axis=0
    )
    own[...] = jnp.zeros_like(own)
    mine = [pick(jnp.minimum(k, held - 1)) for k in range(most)]
    own[:, :rows] = stack([*mine, jnp.minimum(length, held * page)], FIELDS)


def project_queries(message, w_uk, queries, heads, latent, narrow):
    rows = message.shape[0]
    nope = w_uk.shape[1]
    tiles = latent // LANES
    low = lax.broadcasted_iota(jnp.int32, (rows, LANES), 1) < LANES // 2
    for h in range(heads):
        lat = jnp.dot(
            message[:, h * nope : (h + 1) * nope], w_uk[h], preferred_element_type=jnp.float32
        )
        for c in range(tiles):
            queries[c, pl.ds(h, rows, stride=heads), :] = lat[:, c * LANES : (c + 1) * LANES]
    for c in range(narrow // LANES):
        pair = lane_tile(message, heads * nope // LANES + c).astype(jnp.float32)
        swapped = pltpu.roll(pair, LANES // 2, 1)
        for h, left, right in ((2 * c, pair, swapped), (2 * c + 1, swapped, pair)):
            at = pl.ds(h, rows, stride=heads)
            queries[tiles, at, :] = jnp.where(low, left, 0.0)
            queries[tiles + 1, at, :] = jnp.where(low, 0.0, right)


def to_table(moved, count, rows, heads, score_row=None):
    whole = moved.astype(jnp.int32)
    request = whole[ROW : ROW + 1, :]
    query_row = jnp.where(request == 0, rows, request - 1) * heads
    blocks = lax.shift_right_logical(
        count[0:1, :].astype(jnp.int32) + (UNROLL - 1), UNROLL.bit_length() - 1
    )
    row = lax.broadcasted_iota(jnp.int32, whole.shape, 0)
    for k, value in ((ROW, query_row), (COUNT, blocks)):
        whole = jnp.where(row == k, jnp.broadcast_to(value, whole.shape), whole)
    extra = query_row if score_row is None else query_row + score_row(whole)
    return jnp.where(row == SCORE_ROW, jnp.broadcast_to(extra, whole.shape), whole)


def rope_lanes(page, heads):
    quarter = page // 4
    lane = lax.broadcasted_iota(jnp.int32, (heads, LEND * page), 1)
    return lane // page * quarter + lax.rem(lane, page) // 4, lax.rem(lane, 4)


def latent_scores(queries, pool, items, heads):
    tiles = queries.shape[0] - 2
    left, rows = [], []
    for start, slots in items:
        at = pl.ds(start, heads)
        left.append(jnp.concatenate([queries[c, at, :] for c in range(tiles)], axis=1))
        rows += [pool[s] for s in slots]
    parts = lax.dot_general(
        jnp.concatenate(left, axis=0).astype(jnp.bfloat16),
        jnp.concatenate(rows, axis=0),
        (((1,), (1,)), ((), ())),
        preferred_element_type=jnp.float32,
    )
    columns = parts.shape[1] // len(items)
    for i in range(len(items)):
        yield parts[i * heads : (i + 1) * heads, i * columns : (i + 1) * columns]


def rope_scores(queries, rope_keys, items, lanes, heads):
    tiles = queries.shape[0] - 2
    left, rows = [], []
    for start, slots in items:
        turned = jnp.concatenate(
            [queries[tiles, pl.ds(start, heads), :], queries[tiles + 1, pl.ds(start, heads), :]],
            axis=0,
        ).astype(jnp.bfloat16)
        none = jnp.zeros_like(turned)
        left.append(jnp.concatenate([turned, none], axis=1))
        left.append(jnp.concatenate([none, turned], axis=1))
        rows += [rope_keys[s] for s in slots]
    parts = lax.dot_general(
        jnp.concatenate(left, axis=0),
        jnp.concatenate(rows, axis=0),
        (((1,), (1,)), ((), ())),
        preferred_element_type=jnp.float32,
    )
    source, which = lanes
    columns = parts.shape[1] // len(items)
    for i in range(len(items)):
        for j in range(4):
            first = (4 * i + j) * heads
            moved = jnp.take_along_axis(
                parts[first : first + heads, :], source + i * columns, axis=1
            )
            found = moved if j == 0 else jnp.where(which == j, moved, found)
        yield found


def fetch_rows(items, plan, sems):
    copies = [
        pltpu.make_async_copy(items.at[k], plan.at[pl.ds(k * LANES, LANES)], sems.at[k])
        for k in range(TABLE_ROWS)
    ]
    for copy in copies:
        copy.start()
    return copies


def read(plan, row, at):
    return plan[row * LANES + at]


def item(plan, at, heads):
    slots = [read(plan, k, at) for k in range(LEND)]
    return pl.multiple_of(read(plan, ROW, at), heads), slots


def score_work(queries, pool, rope_keys, scores, plan, base, heads, scale):
    page = pool.shape[1]
    scores[...] = jnp.full_like(scores, FAR)
    position = lax.broadcasted_iota(jnp.int32, (heads, LEND * page), 1)
    lanes = rope_lanes(page, heads)
    together = LANES // (LEND * (page // 4))

    @pl.loop(0, read(plan, COUNT, base))
    def _(block):
        first_item = base + block * UNROLL
        items = [item(plan, first_item + u, heads) for u in range(UNROLL)]
        ropes = []
        for first in range(0, UNROLL, together):
            ropes += rope_scores(queries, rope_keys, items[first : first + together], lanes, heads)
        for first in range(0, UNROLL, PAIR):
            mains = latent_scores(queries, pool, items[first : first + PAIR], heads)
            for u, main in enumerate(mains, first):
                start = pl.multiple_of(read(plan, SCORE_ROW, first_item + u), heads)
                scores[pl.ds(start, heads), :] = jnp.where(
                    position < read(plan, LIVE, first_item + u), (main + ropes[u]) * scale, FAR
                )


def soften(scores, weights, norm, lse, total_rows):
    pitch = total_rows + (scores.shape[0] % total_rows) // (scores.shape[0] // total_rows)
    units = scores.shape[0] // pitch
    step = 64
    for r in range(0, total_rows, step):
        block = [scores[j * pitch + r : j * pitch + r + step, :] for j in range(units)]
        top = block[0]
        for one in block[1:]:
            top = jnp.maximum(top, one)
        peak = jnp.max(top, axis=-1, keepdims=True)
        total = jnp.zeros((step, LANES), jnp.float32)
        for j in range(units):
            rounded = jnp.exp(block[j] - peak).astype(jnp.bfloat16).astype(jnp.float32)
            weights[j * pitch + r : j * pitch + r + step, :] = rounded
            total = total + rounded
        total = jnp.sum(total, axis=-1, keepdims=True)
        norm[r : r + step, :] = jnp.broadcast_to(1.0 / total, (step, LANES))
        lse[r : r + step, :] = jnp.broadcast_to(peak + jnp.log(total), (step, LANES))


def value_work(pool, weights, context, plan, base, heads, add):
    @pl.loop(0, read(plan, COUNT, base))
    def _(block):
        for first in range(0, UNROLL, PAIR):
            starts, left, values = [], [], []
            for u in range(first, first + PAIR):
                at = base + block * UNROLL + u
                start, slots = item(plan, at, heads)
                starts.append(start)
                mine = weights[pl.ds(pl.multiple_of(read(plan, SCORE_ROW, at), heads), heads), :]
                none = jnp.zeros_like(mine)
                left.append(
                    jnp.concatenate(
                        [mine if k == u - first else none for k in range(PAIR)], axis=1
                    )
                )
                values += [pool[s] for s in slots]
            summed = jnp.dot(
                jnp.concatenate(left, axis=0).astype(jnp.bfloat16),
                jnp.concatenate(values, axis=0),
                preferred_element_type=jnp.float32,
            )
            for k, start in enumerate(starts):
                for c in range(context.shape[0]):
                    part = summed[k * heads : (k + 1) * heads, c * LANES : (c + 1) * LANES]
                    if add:
                        part = part + context[c, pl.ds(start, heads), :]
                    context[c, pl.ds(start, heads), :] = part


def head_outs(context, norm, w_uv, rows, heads):
    width = w_uv.shape[2]
    for h in range(0, heads, 2):
        pair = []
        for k in range(2):
            at = pl.ds(h + k, rows, stride=heads)
            scale = norm[at, :]
            pair.append(
                jnp.concatenate([context[c, at, :] * scale for c in range(context.shape[0])], axis=1)
            )
        both = jnp.dot(
            jnp.concatenate(pair, axis=0).astype(jnp.bfloat16),
            jnp.concatenate([w_uv[h], w_uv[h + 1]], axis=1),
            preferred_element_type=jnp.float32,
        )
        yield h, both[:rows, :width]
        yield h + 1, both[rows:, width:]


def own_scores_kernel(
    own, message, rope_hbm, pool_hbm, w_uk_hbm,
    pool, rope_keys, weights, norm, lse, items,
    queries, scores, spread, rope_pages, w_uk, fields, plan, sems, plan_sem,
    *, heads, narrow, most,
):
    slots, page, latent = pool.shape
    rows = message.shape[0]
    units = most // LEND
    scale = 1.0 / math.sqrt(w_uk.shape[1] + narrow // heads)
    routes = ((rope_hbm, rope_pages), (w_uk_hbm, w_uk), (pool_hbm, pool))
    fetches = [pltpu.make_async_copy(*route, sems.at[k]) for k, route in enumerate(routes)]
    for fetch in fetches:
        fetch.start()
    tokens = LEND * page
    fields[...] = jnp.zeros_like(fields)
    request = lax.broadcasted_iota(jnp.int32, (1, rows), 1)
    for j in range(units):
        live = jnp.clip(own[most : most + 1, :rows] - j * tokens, 0, tokens)
        values = [own[j * LEND + k : j * LEND + k + 1, :rows] for k in range(LEND)]
        values += [request + 1, live, jnp.zeros_like(live), jnp.full_like(live, j)]
        for k, value in enumerate(values):
            fields[k : k + 1, j * rows : (j + 1) * rows] = value.astype(jnp.float32)
    moved, count = compact(fields[...], LIVE, LANES, LANES)
    pitch = (rows + 1) * heads
    items[...] = to_table(moved, count, rows, heads, lambda w: w[SCORE_ROW : SCORE_ROW + 1, :] * pitch)
    table = fetch_rows(items, plan, plan_sem)
    fetches[0].wait()
    pieces = page // 2
    spacing = pieces + 1
    for c in range(pieces):
        spread[pl.ds(c, slots, stride=spacing), :] = lane_tile(rope_pages, c).astype(jnp.float32)
    for s in range(slots):
        for side in range(2):
            rows_of = spread[pl.ds(s * spacing + side, pieces // 2, stride=2), :]
            rope_keys[s, :, side * LANES : (side + 1) * LANES] = rows_of.astype(jnp.bfloat16)
    fetches[1].wait()
    project_queries(message, w_uk, queries, heads, latent, narrow)
    for copy in table:
        copy.wait()
    fetches[2].wait()
    score_work(queries, pool, rope_keys, scores, plan, 0, heads, scale)
    soften(scores, weights, norm, lse, rows * heads)


def own_values_kernel(items, pool, weights, norm, w_uv, outs, context, plan, plan_sem, *, heads):
    rows = outs.shape[0]
    table = fetch_rows(items, plan, plan_sem)
    context[...] = jnp.zeros_like(context)
    for copy in table:
        copy.wait()
    value_work(pool, weights, context, plan, 0, heads, True)
    width = w_uv.shape[2]
    for h, out in head_outs(context, norm, w_uv, rows, heads):
        outs[:, h * width : (h + 1) * width] = out


def serve_kernel(
    message, pool, rope_keys, w_uk, w_uv, back,
    queries, scores, weights, norm, lse, context, items, plan, plan_sem,
    *, narrow, base,
):
    rows = message.shape[0]
    slots, page, latent = pool.shape
    heads = w_uk.shape[0]
    scale = 1.0 / math.sqrt(w_uk.shape[1] + narrow // heads)
    asked = message[0:FIELDS, message.shape[1] - LANES :].astype(jnp.float32)
    items[...] = to_table(asked, asked[COUNT : COUNT + 1, :], rows, heads)
    table = fetch_rows(items, plan, plan_sem)
    context[...] = jnp.zeros_like(context)
    project_queries(message, w_uk, queries, heads, latent, narrow)
    for copy in table:
        copy.wait()
    score_work(queries, pool, rope_keys, scores, plan, base, heads, scale)
    soften(scores, weights, norm, lse, rows * heads)
    value_work(pool, weights, context, plan, base, heads, False)
    width = w_uv.shape[2]
    lane = lax.broadcasted_iota(jnp.int32, (rows, LANES), 1)
    logs = jnp.zeros((rows, LANES), jnp.float32)
    for h, out in head_outs(context, norm, w_uv, rows, heads):
        back[:, h * width : (h + 1) * width] = out.astype(jnp.bfloat16)
        logs = jnp.where(lax.rem(lane, heads) == h, lse[pl.ds(h, rows, stride=heads), :], logs)
    packed = jnp.zeros((rows, LANES), jnp.float32)
    for part in range(3):
        piece = logs.astype(jnp.bfloat16).astype(jnp.float32)
        logs = logs - piece
        packed = jnp.where(lane // heads == part, piece, packed)
    back[:, heads * width :] = packed.astype(jnp.bfloat16)


def join_kernel(outs, lse, from_a, from_b, w_o, sent, kept, joined, *, heads):
    rows = outs.shape[0]
    width = outs.shape[1] // heads
    totals = []
    for arrived in (from_a, from_b):
        tile = arrived[:, heads * width :].astype(jnp.float32)
        total = tile + pltpu.roll(tile, LANES - heads, 1) + pltpu.roll(tile, LANES - 2 * heads, 1)
        totals.append(total)
    for h in range(heads):
        at = slice(h * width, (h + 1) * width)
        logs = [lse[pl.ds(h, rows, stride=heads), :]]
        values = [outs[:, at]]
        for arrived, total in zip((from_a, from_b), totals):
            logs.append(jnp.broadcast_to(total[:, h : h + 1], (rows, LANES)))
            values.append(arrived[:, at].astype(jnp.float32))
        peak = jnp.maximum(jnp.maximum(logs[0], logs[1]), logs[2])
        shares = [jnp.exp(one - peak) for one in logs]
        top = shares[0] * values[0] + shares[1] * values[1] + shares[2] * values[2]
        joined[:, at] = (top / (shares[0] + shares[1] + shares[2])).astype(jnp.bfloat16)
    mine = lax.axis_index("tp")
    other = lax.rem(mine + 1, lax.axis_size("tp"))
    cols = sent.shape[1]
    heads_joined = joined[...]
    away = pl.ds(pl.multiple_of(other * cols, cols), cols)
    here = pl.ds(pl.multiple_of(mine * cols, cols), cols)
    sent[...] = jnp.dot(
        heads_joined, w_o[:, away], preferred_element_type=jnp.float32
    ).astype(jnp.bfloat16)
    kept[...] = jnp.dot(heads_joined, w_o[:, here], preferred_element_type=jnp.float32)


def vmem():
    return pl.BlockSpec(memory_space=pltpu.VMEM)


def in_hbm(array):
    return pltpu.with_memory_space_constraint(array, pltpu.HBM)


def call(kernel, name, out, ins, scratch, limit, cost=None, **sizes):
    return pl.pallas_call(
        functools.partial(kernel, **sizes),
        name=name,
        out_shape=out,
        in_specs=ins,
        out_specs=jax.tree.map(lambda _: vmem(), out),
        scratch_shapes=scratch,
        compiler_params=pltpu.CompilerParams(vmem_limit_bytes=limit * MIB),
        cost_estimate=cost,
    )


def shards(
    q_nope, q_rope, lengths, page_table, lend_counts, latent_pages, rope_pages, w_uk, w_uv, w_o
):
    rows = lengths.shape[0]
    heads, nope, latent = w_uk.shape
    slots, page, _ = latent_pages.shape
    most = page_table.shape[1]
    width = w_uv.shape[2]
    narrow = q_rope.shape[1]
    tiles = latent // LANES
    units = most // LEND
    assert rows * units <= LANES and FIELDS <= rows <= LANES // 2 and page * LEND == LANES
    f32, bf16, i32 = jnp.float32, jnp.bfloat16, jnp.int32
    shape = jax.ShapeDtypeStruct
    sem = pltpu.SemaphoreType.DMA
    stats = (rows * heads, LANES)
    padded = (rows + 1) * heads
    block = pltpu.VMEM((tiles + 2, padded, LANES), f32)
    contexts = pltpu.VMEM((tiles, padded, LANES), f32)
    plan = pltpu.SMEM((TABLE_ROWS * LANES,), i32)

    message, own = call(
        pack_kernel,
        "pack",
        (shape((rows, heads * nope + narrow + LANES), bf16), shape((FIELDS, LANES), i32)),
        [vmem()] * 5,
        [pltpu.VMEM((FIELDS, LANES), f32)],
        4,
        page=page,
    )(*map(in_hbm, (lengths.reshape(1, rows), page_table.T, lend_counts.T, q_nope, q_rope)))
    asked_a = swap(message, "dp", False)
    asked_b = swap(message, "dp", True)

    pool, rope_keys, weights, norm, lse, items = call(
        own_scores_kernel,
        "own_scores",
        (
            shape((slots, page, latent), bf16),
            shape((slots, page // 4, 2 * LANES), bf16),
            shape((units * padded, LANES), f32),
            shape(stats, f32),
            shape(stats, f32),
            shape((FIELDS, LANES), i32),
        ),
        [vmem()] * 2 + [pl.BlockSpec(memory_space=pl.ANY)] * 3,
        [
            block,
            pltpu.VMEM((units * padded, LANES), f32),
            pltpu.VMEM((slots * (page // 2 + 1), LANES), f32),
            pltpu.VMEM(rope_pages.shape, bf16),
            pltpu.VMEM(w_uk.shape, bf16),
            pltpu.VMEM((FIELDS, LANES), f32),
            plan,
            sem((3,)),
            sem((TABLE_ROWS,)),
        ],
        24,
        pl.CostEstimate(
            flops=2 * rows * heads * most * page * (latent + LANES),
            bytes_accessed=slots * page * (latent + LANES) * 2,
            transcendentals=rows * heads * most * page,
        ),
        heads=heads,
        narrow=narrow,
        most=most,
    )(own, message, *map(in_hbm, (rope_pages, latent_pages, w_uk)))

    serve_scratch = [
        block,
        pltpu.VMEM((padded, LANES), f32),
        pltpu.VMEM((padded, LANES), f32),
        pltpu.VMEM(stats, f32),
        pltpu.VMEM(stats, f32),
        contexts,
        pltpu.VMEM((FIELDS, LANES), i32),
        plan,
        sem((TABLE_ROWS,)),
    ]

    def serve(asked, name, base):
        return call(
            serve_kernel,
            name,
            shape((rows, heads * width + LANES), bf16),
            [vmem()] * 5,
            serve_scratch,
            8,
            narrow=narrow,
            base=base,
        )(asked, pool, rope_keys, w_uk, w_uv)

    from_b = swap(serve(asked_b, "serve_b", LANES // 2), "dp", True)
    from_a = swap(serve(asked_a, "serve_a", 0), "dp", False)
    outs = call(
        own_values_kernel,
        "own_values",
        shape((rows, heads * width), f32),
        [vmem()] * 5,
        [contexts, plan, sem((TABLE_ROWS,))],
        8,
        heads=heads,
    )(items, pool, weights, norm, w_uv)
    cols = w_o.shape[1] // lax.axis_size("tp")
    sent, kept = call(
        join_kernel,
        "join",
        (shape((rows, cols), bf16), shape((rows, cols), f32)),
        [vmem()] * 5,
        [pltpu.VMEM((rows, heads * width), bf16)],
        8,
        heads=heads,
    )(outs, lse, from_a, from_b, w_o)
    return (kept + swap(sent, "tp", False).astype(f32)).astype(bf16)


def solution(mesh):
    in_specs = (
        P("dp", "tp"),
        P("dp", "tp"),
        P("dp"),
        P("dp", None),
        P("dp", None),
        P("dp", None, None),
        P("dp", None),
        P("tp", None, None),
        P("tp", None, None),
        P("tp", None),
    )
    out_specs = P("dp", "tp")
    return jax.shard_map(shards, mesh=mesh, in_specs=in_specs, out_specs=out_specs, check_vma=False)
```

```python
import functools
import math

import jax
import jax.numpy as jnp
from jax import lax
from jax.experimental import pallas as pl
from jax.experimental.pallas import tpu as pltpu
from jax.sharding import PartitionSpec as P

LEND = 2
LANES = 128
FIELDS = 16
ROW, LIVE, COUNT, UNIT, LIVE_OF = 2, 3, 4, 5, 6
LANE, TOKEN_ROW, WEIGHT_ROW = 3, 5, 6
TABLE_ROWS = 7
FAR = -1e30
UNROLL = 8
PAIR = 2
MIB = 1 << 20


def swap(block, axis, odd_first):
    count = lax.axis_size(axis)
    shift = 1 if odd_first else 0
    pairs = []
    for start in range(shift, count + shift, 2):
        a, b = start % count, (start + 1) % count
        pairs += [(a, b), (b, a)]
    return lax.ppermute(block, axis, pairs)


def lane_tile(ref, index):
    return ref[:, index * LANES : (index + 1) * LANES]


def compact(fields, live_row, segment, spacing):
    height, lanes = fields.shape
    row = lax.broadcasted_iota(jnp.int32, (lanes, lanes), 0)
    column = lax.broadcasted_iota(jnp.int32, (lanes, lanes), 1)
    kept = jnp.where(fields[live_row : live_row + 1, :] > 0.0, 1.0, 0.0)
    kept = jnp.broadcast_to(kept, (height, lanes))
    ahead = (row // segment == column // segment) & (row < column)
    inside = row // segment == column // spacing
    place = jnp.dot(
        kept.astype(jnp.bfloat16),
        jnp.where(ahead, 1.0, 0.0).astype(jnp.bfloat16),
        preferred_element_type=jnp.float32,
    )
    count = jnp.dot(
        kept.astype(jnp.bfloat16),
        jnp.where(inside, 1.0, 0.0).astype(jnp.bfloat16),
        preferred_element_type=jnp.float32,
    )
    lane = lax.broadcasted_iota(jnp.int32, (height, lanes), 1)
    target = place.astype(jnp.int32) + lane // segment * spacing
    target = jnp.where(kept > 0.0, target, -1)
    chosen = jnp.where(jnp.broadcast_to(target[0:1, :], (lanes, lanes)) == row, 1.0, 0.0)
    moved = lax.dot_general(
        fields.astype(jnp.bfloat16),
        chosen.astype(jnp.bfloat16),
        (((1,), (1,)), ((), ())),
        preferred_element_type=jnp.float32,
    )
    return moved, count


def pack_kernel(lengths, table, lend, q_nope, q_rope, message, own, fields, *, page, heads):
    rows = q_nope.shape[0]
    most = table.shape[0]
    shift = page.bit_length() - 1
    wide, narrow = q_nope.shape[1], q_rope.shape[1]
    length = lengths[...]
    count = lax.shift_right_logical(length + (page - 1), shift)
    to_prev, to_next = lend[0:1, :], lend[1:2, :]
    held = count - to_prev - to_next
    request = lax.broadcasted_iota(jnp.int32, (1, rows), 1)

    def pick(index):
        found = jnp.zeros_like(index)
        for k in range(most):
            found = jnp.where(index == k, table[k : k + 1, :], found)
        return found

    def lent(first, number):
        slots = [pick(jnp.minimum(first + k, count - 1)) for k in range(LEND)]
        live = jnp.minimum(length - first * page, number * page)
        return [*slots, request + 1, jnp.maximum(live, 0)]

    def stack(values, height):
        row = lax.broadcasted_iota(jnp.int32, (height, rows), 0)
        block = jnp.zeros((height, rows), jnp.int32)
        for k, value in enumerate(values):
            block = jnp.where(row == k, jnp.broadcast_to(value, (height, rows)), block)
        return block

    prev, nxt = lent(held, to_prev), lent(count - to_next, to_next)
    odd = lax.rem(lax.axis_index("dp"), 2) == 1
    fields[...] = jnp.zeros_like(fields)
    for k, (yes, no) in enumerate(((prev, nxt), (nxt, prev))):
        mine = stack([jnp.where(odd, p, n) for p, n in zip(yes, no)], FIELDS)
        fields[:, k * rows : (k + 1) * rows] = mine.astype(jnp.float32)
    moved, counts = compact(fields[...], LIVE, LANES // heads, LANES // (2 * rows * heads // LANES))
    row = lax.broadcasted_iota(jnp.int32, (FIELDS, LANES), 0)
    live_of = jnp.broadcast_to(fields[LIVE : LIVE + 1, :], (FIELDS, LANES))
    asked = jnp.where(row == COUNT, counts, jnp.where(row == LIVE_OF, live_of, moved))
    asked = asked.astype(message.dtype)
    message[:, :wide] = q_nope[...]
    message[:, wide : wide + narrow] = q_rope[...]
    message[:, wide + narrow :] = jnp.concatenate(
        [asked, jnp.zeros((rows - FIELDS, LANES), message.dtype)], axis=0
    )
    own[...] = jnp.zeros_like(own)
    mine = [pick(jnp.minimum(k, held - 1)) for k in range(most)]
    own[:, :rows] = stack([*mine, jnp.minimum(length, held * page)], FIELDS)


def project_queries(message, w_uk, spread, queries, heads, latent, narrow):
    rows = message.shape[0]
    nope = w_uk.shape[1]
    tiles = latent // LANES
    low = lax.broadcasted_iota(jnp.int32, (rows, LANES), 1) < LANES // 2
    for h in range(heads):
        lat = jnp.dot(
            message[:, h * nope : (h + 1) * nope], w_uk[h], preferred_element_type=jnp.float32
        )
        for c in range(tiles):
            spread[c, pl.ds(h, rows, stride=heads), :] = lat[:, c * LANES : (c + 1) * LANES]
    for c in range(narrow // LANES):
        pair = lane_tile(message, heads * nope // LANES + c).astype(jnp.float32)
        swapped = pltpu.roll(pair, LANES // 2, 1)
        spread[tiles, pl.ds(2 * c, rows, stride=heads), :] = jnp.where(low, pair, swapped)
        spread[tiles, pl.ds(2 * c + 1, rows, stride=heads), :] = jnp.where(low, swapped, pair)
    for c in range(tiles + 1):
        queries[:, c * LANES : (c + 1) * LANES] = spread[c].astype(jnp.bfloat16)


def to_table(moved, count, rows, heads, pitch):
    whole = moved.astype(jnp.int32)
    group_rows = LANES // heads
    groups = rows // group_rows
    request = whole[ROW : ROW + 1, :] - 1
    unit = whole[UNIT : UNIT + 1, :]
    idle = request < 0
    query_row = jnp.where(idle, rows, request) * heads
    group = jnp.where(idle, 0, request) // group_rows
    blocks = lax.shift_right_logical(
        count[0:1, :].astype(jnp.int32) + (UNROLL - 1), UNROLL.bit_length() - 1
    )
    row = lax.broadcasted_iota(jnp.int32, whole.shape, 0)
    for k, value in (
        (ROW, query_row),
        (LANE, jnp.where(idle, LANES, query_row - group * LANES)),
        (COUNT, blocks),
        (TOKEN_ROW, (unit * groups + group) * LANES),
        (WEIGHT_ROW, query_row + unit * pitch),
    ):
        whole = jnp.where(row == k, jnp.broadcast_to(value, whole.shape), whole)
    return whole


def live_lanes(live, first, rows, heads):
    high = lax.shift_right_logical(live, LANES.bit_length() - 1)
    low = live & (LANES - 1)
    row = lax.broadcasted_iota(jnp.int32, (8, LANES), 0)
    halves = jnp.where(row == 0, jnp.broadcast_to(high, (8, LANES)), jnp.broadcast_to(low, (8, LANES)))
    source = lax.broadcasted_iota(jnp.int32, (LANES, LANES), 0)
    lane = lax.broadcasted_iota(jnp.int32, (LANES, LANES), 1)
    found = []
    for g in range(rows * heads // LANES):
        chosen = jnp.where(source == first + (g * LANES + lane) // heads, 1.0, 0.0)
        spread = jnp.dot(
            halves.astype(jnp.float32).astype(jnp.bfloat16),
            chosen.astype(jnp.bfloat16),
            preferred_element_type=jnp.float32,
        ).astype(jnp.int32)
        found.append(spread[0:1, :] * LANES + spread[1:2, :])
    return found


def fetch_rows(items, plan, sems):
    copies = [
        pltpu.make_async_copy(items.at[k], plan.at[pl.ds(k * LANES, LANES)], sems.at[k])
        for k in range(TABLE_ROWS)
    ]
    for copy in copies:
        copy.start()
    return copies


def read(plan, row, at):
    return plan[row * LANES + at]


def score_work(queries, pool, rope_keys, scores, plan, bases, heads):
    tokens = LEND * pool.shape[1]
    lane = lax.broadcasted_iota(jnp.int32, (tokens, LANES), 1)
    for g, base in enumerate(bases):

        @pl.loop(0, read(plan, COUNT, base))
        def _(block):
            first = base + block * UNROLL
            keys = []
            for u in range(UNROLL):
                for k in range(LEND):
                    s = read(plan, k, first + u)
                    keys.append(jnp.concatenate([pool[s], rope_keys[s]], axis=1))
            found = lax.dot_general(
                jnp.concatenate(keys, axis=0),
                queries[g * LANES : (g + 1) * LANES, :],
                (((1,), (1,)), ((), ())),
                preferred_element_type=jnp.float32,
            )
            for u in range(UNROLL):
                start = read(plan, LANE, first + u)
                mine = (lane >= start) & (lane < start + heads)
                at = pl.ds(pl.multiple_of(read(plan, TOKEN_ROW, first + u), LANES), tokens)
                pltpu.store(
                    scores.at[at, :], found[u * tokens : (u + 1) * tokens, :], mask=mine
                )


def soften(scores, weights, norm, lse, lives, scale, pitch):
    groups = len(lives)
    units = scores.shape[0] // (groups * LANES)
    step = 32
    for g, live in enumerate(lives):
        token = lax.broadcasted_iota(jnp.int32, (step, LANES), 0)
        top = jnp.full((step, LANES), FAR, jnp.float32)
        for j in range(units):
            for r in range(0, LANES, step):
                at = slice((j * groups + g) * LANES + r, (j * groups + g) * LANES + r + step)
                one = jnp.where(token + (j * LANES + r) < live, scores[at, :] * scale, FAR)
                scores[at, :] = one
                top = jnp.maximum(top, one)
        peak = jnp.max(top, axis=0, keepdims=True)
        total = jnp.zeros((step, LANES), jnp.float32)
        for j in range(units):
            for r in range(0, LANES, step):
                at = slice((j * groups + g) * LANES + r, (j * groups + g) * LANES + r + step)
                rounded = jnp.exp(scores[at, :] - peak).astype(jnp.bfloat16).astype(jnp.float32)
                scores[at, :] = rounded
                total = total + rounded
        total = jnp.sum(total, axis=0, keepdims=True)
        here = slice(g * LANES, (g + 1) * LANES)
        norm[here, :] = jnp.transpose(jnp.broadcast_to(1.0 / total, (LANES, LANES)))
        lse[here, :] = jnp.transpose(jnp.broadcast_to(peak + jnp.log(total), (LANES, LANES)))
        for j in range(units):
            at = slice((j * groups + g) * LANES, (j * groups + g + 1) * LANES)
            weights[j * pitch + g * LANES : j * pitch + (g + 1) * LANES, :] = jnp.transpose(
                scores[at, :]
            )


def value_work(pool, weights, context, plan, bases, heads, add):
    for base in bases:

        @pl.loop(0, read(plan, COUNT, base))
        def _(block):
            for first in range(0, UNROLL, PAIR):
                starts, left, values = [], [], []
                for u in range(first, first + PAIR):
                    at = base + block * UNROLL + u
                    starts.append(pl.multiple_of(read(plan, ROW, at), heads))
                    from_row = pl.multiple_of(read(plan, WEIGHT_ROW, at), heads)
                    mine = weights[pl.ds(from_row, heads), :]
                    none = jnp.zeros_like(mine)
                    left.append(
                        jnp.concatenate(
                            [mine if k == u - first else none for k in range(PAIR)], axis=1
                        )
                    )
                    values += [pool[read(plan, k, at)] for k in range(LEND)]
                summed = jnp.dot(
                    jnp.concatenate(left, axis=0).astype(jnp.bfloat16),
                    jnp.concatenate(values, axis=0),
                    preferred_element_type=jnp.float32,
                )
                for k, start in enumerate(starts):
                    for c in range(context.shape[0]):
                        part = summed[k * heads : (k + 1) * heads, c * LANES : (c + 1) * LANES]
                        if add:
                            part = part + context[c, pl.ds(start, heads), :]
                        context[c, pl.ds(start, heads), :] = part


def head_outs(context, norm, w_uv, rows, heads):
    width = w_uv.shape[2]
    for h in range(0, heads, 2):
        pair = []
        for k in range(2):
            at = pl.ds(h + k, rows, stride=heads)
            scale = norm[at, :]
            pair.append(
                jnp.concatenate([context[c, at, :] * scale for c in range(context.shape[0])], axis=1)
            )
        both = jnp.dot(
            jnp.concatenate(pair, axis=0).astype(jnp.bfloat16),
            jnp.concatenate([w_uv[h], w_uv[h + 1]], axis=1),
            preferred_element_type=jnp.float32,
        )
        yield h, both[:rows, :width]
        yield h + 1, both[rows:, width:]


def own_scores_kernel(
    own, message, rope_hbm, pool_hbm, w_uk_hbm,
    pool, rope_keys, weights, norm, lse, items,
    apart, queries, scores, spread, rope_pages, w_uk, fields, plan, sems, plan_sem,
    *, heads, narrow, most,
):
    slots, page, latent = pool.shape
    rows = message.shape[0]
    units = most // LEND
    scale = 1.0 / math.sqrt(w_uk.shape[1] + narrow // heads)
    routes = ((rope_hbm, rope_pages), (w_uk_hbm, w_uk), (pool_hbm, pool))
    fetches = [pltpu.make_async_copy(*route, sems.at[k]) for k, route in enumerate(routes)]
    for fetch in fetches:
        fetch.start()
    tokens = LEND * page
    fields[...] = jnp.zeros_like(fields)
    request = lax.broadcasted_iota(jnp.int32, (1, rows), 1)
    group_rows = LANES // heads
    groups = rows // group_rows
    for j in range(units):
        live = jnp.clip(own[most : most + 1, :rows] - j * tokens, 0, tokens)
        values = [own[j * LEND + k : j * LEND + k + 1, :rows] for k in range(LEND)]
        values += [request + 1, live, jnp.zeros_like(live), jnp.full_like(live, j)]
        for k, value in enumerate(values):
            for g in range(groups):
                first = (g * units + j) * group_rows
                fields[k : k + 1, first : first + group_rows] = value[
                    :, g * group_rows : (g + 1) * group_rows
                ].astype(jnp.float32)
    moved, count = compact(fields[...], LIVE, LANES // groups, LANES // groups)
    pitch = (rows + 1) * heads
    items[...] = to_table(moved, count, rows, heads, pitch)
    lives = live_lanes(own[most : most + 1, :], 0, rows, heads)
    table = fetch_rows(items, plan, plan_sem)
    fetches[0].wait()
    low = lax.broadcasted_iota(jnp.int32, (slots, LANES), 1) < LANES // 2
    for c in range(page // 2):
        pair = lane_tile(rope_pages, c).astype(jnp.float32)
        spread[pl.ds(2 * c, slots, stride=page + 1), :] = jnp.where(low, pair, 0.0)
        spread[pl.ds(2 * c + 1, slots, stride=page + 1), :] = jnp.where(low, 0.0, pair)
    for s in range(slots):
        first = s * (page + 1)
        rope_keys[s] = spread[first : first + page, :].astype(jnp.bfloat16)
    fetches[1].wait()
    project_queries(message, w_uk, apart, queries, heads, latent, narrow)
    for copy in table:
        copy.wait()
    fetches[2].wait()
    bases = [g * (LANES // groups) for g in range(groups)]
    score_work(queries, pool, rope_keys, scores, plan, bases, heads)
    soften(scores, weights, norm, lse, lives, scale, pitch)


def own_values_kernel(items, pool, weights, norm, w_uv, outs, context, plan, plan_sem, *, heads):
    rows = outs.shape[0]
    table = fetch_rows(items, plan, plan_sem)
    context[...] = jnp.zeros_like(context)
    for copy in table:
        copy.wait()
    groups = rows * heads // LANES
    bases = [g * (LANES // groups) for g in range(groups)]
    value_work(pool, weights, context, plan, bases, heads, True)
    width = w_uv.shape[2]
    for h, out in head_outs(context, norm, w_uv, rows, heads):
        outs[:, h * width : (h + 1) * width] = out


def serve_kernel(
    message, pool, rope_keys, w_uk, w_uv, back,
    apart, queries, scores, weights, norm, lse, context, items, plan, plan_sem,
    *, narrow, side,
):
    rows = message.shape[0]
    slots, page, latent = pool.shape
    heads = w_uk.shape[0]
    scale = 1.0 / math.sqrt(w_uk.shape[1] + narrow // heads)
    asked = message[0:FIELDS, message.shape[1] - LANES :].astype(jnp.float32)
    unit = lax.broadcasted_iota(jnp.int32, asked.shape, 0) == UNIT
    items[...] = to_table(
        jnp.where(unit, 0.0, asked), asked[COUNT : COUNT + 1, :], rows, heads, 0
    )
    live_of = asked[LIVE_OF : LIVE_OF + 1, :].astype(jnp.int32)
    lives = live_lanes(live_of, side * rows, rows, heads)
    table = fetch_rows(items, plan, plan_sem)
    context[...] = jnp.zeros_like(context)
    project_queries(message, w_uk, apart, queries, heads, latent, narrow)
    for copy in table:
        copy.wait()
    groups = rows * heads // LANES
    bases = [(side * groups + g) * (LANES // (2 * groups)) for g in range(groups)]
    score_work(queries, pool, rope_keys, scores, plan, bases, heads)
    soften(scores, weights, norm, lse, lives, scale, 0)
    value_work(pool, weights, context, plan, bases, heads, False)
    width = w_uv.shape[2]
    lane = lax.broadcasted_iota(jnp.int32, (rows, LANES), 1)
    logs = jnp.zeros((rows, LANES), jnp.float32)
    for h, out in head_outs(context, norm, w_uv, rows, heads):
        back[:, h * width : (h + 1) * width] = out.astype(jnp.bfloat16)
        logs = jnp.where(lax.rem(lane, heads) == h, lse[pl.ds(h, rows, stride=heads), :], logs)
    packed = jnp.zeros((rows, LANES), jnp.float32)
    for part in range(3):
        piece = logs.astype(jnp.bfloat16).astype(jnp.float32)
        logs = logs - piece
        packed = jnp.where(lane // heads == part, piece, packed)
    back[:, heads * width :] = packed.astype(jnp.bfloat16)


def join_kernel(outs, lse, from_a, from_b, w_o, sent, kept, joined, *, heads):
    rows = outs.shape[0]
    width = outs.shape[1] // heads
    totals = []
    for arrived in (from_a, from_b):
        tile = arrived[:, heads * width :].astype(jnp.float32)
        total = tile + pltpu.roll(tile, LANES - heads, 1) + pltpu.roll(tile, LANES - 2 * heads, 1)
        totals.append(total)
    for h in range(heads):
        at = slice(h * width, (h + 1) * width)
        logs = [lse[pl.ds(h, rows, stride=heads), :]]
        values = [outs[:, at]]
        for arrived, total in zip((from_a, from_b), totals):
            logs.append(jnp.broadcast_to(total[:, h : h + 1], (rows, LANES)))
            values.append(arrived[:, at].astype(jnp.float32))
        peak = jnp.maximum(jnp.maximum(logs[0], logs[1]), logs[2])
        shares = [jnp.exp(one - peak) for one in logs]
        top = shares[0] * values[0] + shares[1] * values[1] + shares[2] * values[2]
        joined[:, at] = (top / (shares[0] + shares[1] + shares[2])).astype(jnp.bfloat16)
    mine = lax.axis_index("tp")
    other = lax.rem(mine + 1, lax.axis_size("tp"))
    cols = sent.shape[1]
    heads_joined = joined[...]
    away = pl.ds(pl.multiple_of(other * cols, cols), cols)
    here = pl.ds(pl.multiple_of(mine * cols, cols), cols)
    sent[...] = jnp.dot(
        heads_joined, w_o[:, away], preferred_element_type=jnp.float32
    ).astype(jnp.bfloat16)
    kept[...] = jnp.dot(heads_joined, w_o[:, here], preferred_element_type=jnp.float32)


def vmem():
    return pl.BlockSpec(memory_space=pltpu.VMEM)


def in_hbm(array):
    return pltpu.with_memory_space_constraint(array, pltpu.HBM)


def call(kernel, name, out, ins, scratch, limit, cost=None, **sizes):
    return pl.pallas_call(
        functools.partial(kernel, **sizes),
        name=name,
        out_shape=out,
        in_specs=ins,
        out_specs=jax.tree.map(lambda _: vmem(), out),
        scratch_shapes=scratch,
        compiler_params=pltpu.CompilerParams(vmem_limit_bytes=limit * MIB),
        cost_estimate=cost,
    )


def shards(
    q_nope, q_rope, lengths, page_table, lend_counts, latent_pages, rope_pages, w_uk, w_uv, w_o
):
    rows = lengths.shape[0]
    heads, nope, latent = w_uk.shape
    slots, page, _ = latent_pages.shape
    most = page_table.shape[1]
    width = w_uv.shape[2]
    narrow = q_rope.shape[1]
    tiles = latent // LANES
    units = most // LEND
    assert rows * heads % LANES == 0 and rows * units <= LANES and FIELDS <= rows <= LANES // 2 and page * LEND == LANES
    f32, bf16, i32 = jnp.float32, jnp.bfloat16, jnp.int32
    shape = jax.ShapeDtypeStruct
    sem = pltpu.SemaphoreType.DMA
    stats = (rows * heads, LANES)
    padded = (rows + 1) * heads
    groups = rows * heads // LANES
    apart = pltpu.VMEM((tiles + 1, rows * heads, LANES), f32)
    queries = pltpu.VMEM((rows * heads, latent + LANES), bf16)
    contexts = pltpu.VMEM((tiles, padded, LANES), f32)
    plan = pltpu.SMEM((TABLE_ROWS * LANES,), i32)

    message, own = call(
        pack_kernel,
        "pack",
        (shape((rows, heads * nope + narrow + LANES), bf16), shape((FIELDS, LANES), i32)),
        [vmem()] * 5,
        [pltpu.VMEM((FIELDS, LANES), f32)],
        4,
        page=page,
        heads=heads,
    )(*map(in_hbm, (lengths.reshape(1, rows), page_table.T, lend_counts.T, q_nope, q_rope)))
    asked_a = swap(message, "dp", False)
    asked_b = swap(message, "dp", True)

    pool, rope_keys, weights, norm, lse, items = call(
        own_scores_kernel,
        "own_scores",
        (
            shape((slots, page, latent), bf16),
            shape((slots, page, LANES), bf16),
            shape((units * padded, LANES), f32),
            shape(stats, f32),
            shape(stats, f32),
            shape((FIELDS, LANES), i32),
        ),
        [vmem()] * 2 + [pl.BlockSpec(memory_space=pl.ANY)] * 3,
        [
            apart,
            queries,
            pltpu.VMEM((units * groups * LANES, LANES), f32),
            pltpu.VMEM((slots * (page + 1), LANES), f32),
            pltpu.VMEM(rope_pages.shape, bf16),
            pltpu.VMEM(w_uk.shape, bf16),
            pltpu.VMEM((FIELDS, LANES), f32),
            plan,
            sem((3,)),
            sem((TABLE_ROWS,)),
        ],
        24,
        pl.CostEstimate(
            flops=2 * rows * heads * most * page * (latent + LANES),
            bytes_accessed=slots * page * (latent + LANES) * 2,
            transcendentals=rows * heads * most * page,
        ),
        heads=heads,
        narrow=narrow,
        most=most,
    )(own, message, *map(in_hbm, (rope_pages, latent_pages, w_uk)))

    serve_scratch = [
        apart,
        queries,
        pltpu.VMEM((groups * LANES, LANES), f32),
        pltpu.VMEM((padded, LANES), f32),
        pltpu.VMEM(stats, f32),
        pltpu.VMEM(stats, f32),
        contexts,
        pltpu.VMEM((FIELDS, LANES), i32),
        plan,
        sem((TABLE_ROWS,)),
    ]

    def serve(asked, name, side):
        return call(
            serve_kernel,
            name,
            shape((rows, heads * width + LANES), bf16),
            [vmem()] * 5,
            serve_scratch,
            8,
            narrow=narrow,
            side=side,
        )(asked, pool, rope_keys, w_uk, w_uv)

    from_b = swap(serve(asked_b, "serve_b", 1), "dp", True)
    from_a = swap(serve(asked_a, "serve_a", 0), "dp", False)
    outs = call(
        own_values_kernel,
        "own_values",
        shape((rows, heads * width), f32),
        [vmem()] * 5,
        [contexts, plan, sem((TABLE_ROWS,))],
        8,
        heads=heads,
    )(items, pool, weights, norm, w_uv)
    cols = w_o.shape[1] // lax.axis_size("tp")
    sent, kept = call(
        join_kernel,
        "join",
        (shape((rows, cols), bf16), shape((rows, cols), f32)),
        [vmem()] * 5,
        [pltpu.VMEM((rows, heads * width), bf16)],
        8,
        heads=heads,
    )(outs, lse, from_a, from_b, w_o)
    return (kept + swap(sent, "tp", False).astype(f32)).astype(bf16)


def solution(mesh):
    in_specs = (
        P("dp", "tp"),
        P("dp", "tp"),
        P("dp"),
        P("dp", None),
        P("dp", None),
        P("dp", None, None),
        P("dp", None),
        P("tp", None, None),
        P("tp", None, None),
        P("tp", None),
    )
    out_specs = P("dp", "tp")
    return jax.shard_map(shards, mesh=mesh, in_specs=in_specs, out_specs=out_specs, check_vma=False)
```

```python
import functools
import math

import jax
import jax.numpy as jnp
from jax import lax
from jax.experimental import pallas as pl
from jax.experimental.pallas import tpu as pltpu
from jax.sharding import PartitionSpec as P


LEND = 2
LANES = 128
FIELDS = 16
ROW, LIVE, COUNT, SCORE_ROW = 2, 3, 4, 5
TABLE_ROWS = 6
FAR = -1e30
UNROLL = 8
PAIR = 2
MIB = 1 << 20


def swap(block, axis, odd_first):
    count = lax.axis_size(axis)
    shift = 1 if odd_first else 0
    pairs = []
    for start in range(shift, count + shift, 2):
        a, b = start % count, (start + 1) % count
        pairs += [(a, b), (b, a)]
    return lax.ppermute(block, axis, pairs)


def lane_tile(ref, index):
    return ref[:, index * LANES : (index + 1) * LANES]


def compact(fields, live_row, segment, spacing):
    height, lanes = fields.shape
    row = lax.broadcasted_iota(jnp.int32, (lanes, lanes), 0)
    column = lax.broadcasted_iota(jnp.int32, (lanes, lanes), 1)
    kept = jnp.where(fields[live_row : live_row + 1, :] > 0.0, 1.0, 0.0)
    kept = jnp.broadcast_to(kept, (height, lanes))
    ahead = (row // segment == column // segment) & (row < column)
    inside = row // segment == column // spacing
    place = jnp.dot(
        kept.astype(jnp.bfloat16),
        jnp.where(ahead, 1.0, 0.0).astype(jnp.bfloat16),
        preferred_element_type=jnp.float32,
    )
    count = jnp.dot(
        kept.astype(jnp.bfloat16),
        jnp.where(inside, 1.0, 0.0).astype(jnp.bfloat16),
        preferred_element_type=jnp.float32,
    )
    lane = lax.broadcasted_iota(jnp.int32, (height, lanes), 1)
    target = place.astype(jnp.int32) + lane // segment * spacing
    target = jnp.where(kept > 0.0, target, -1)
    chosen = jnp.where(jnp.broadcast_to(target[0:1, :], (lanes, lanes)) == row, 1.0, 0.0)
    moved = lax.dot_general(
        fields.astype(jnp.bfloat16),
        chosen.astype(jnp.bfloat16),
        (((1,), (1,)), ((), ())),
        preferred_element_type=jnp.float32,
    )
    return moved, count


def pack_kernel(lengths, table, lend, q_nope, q_rope, message, own, fields, *, page):
    rows = q_nope.shape[0]
    most = table.shape[0]
    shift = page.bit_length() - 1
    wide, narrow = q_nope.shape[1], q_rope.shape[1]
    length = lengths[...]
    count = lax.shift_right_logical(length + (page - 1), shift)
    to_prev, to_next = lend[0:1, :], lend[1:2, :]
    held = count - to_prev - to_next
    request = lax.broadcasted_iota(jnp.int32, (1, rows), 1)

    def pick(index):
        found = jnp.zeros_like(index)
        for k in range(most):
            found = jnp.where(index == k, table[k : k + 1, :], found)
        return found

    def lent(first, number):
        slots = [pick(jnp.minimum(first + k, count - 1)) for k in range(LEND)]
        live = jnp.minimum(length - first * page, number * page)
        return [*slots, request + 1, jnp.maximum(live, 0)]

    def stack(values, height):
        row = lax.broadcasted_iota(jnp.int32, (height, rows), 0)
        block = jnp.zeros((height, rows), jnp.int32)
        for k, value in enumerate(values):
            block = jnp.where(row == k, jnp.broadcast_to(value, (height, rows)), block)
        return block

    prev, nxt = lent(held, to_prev), lent(count - to_next, to_next)
    odd = lax.rem(lax.axis_index("dp"), 2) == 1
    fields[...] = jnp.zeros_like(fields)
    for k, (yes, no) in enumerate(((prev, nxt), (nxt, prev))):
        mine = stack([jnp.where(odd, p, n) for p, n in zip(yes, no)], FIELDS)
        fields[:, k * rows : (k + 1) * rows] = mine.astype(jnp.float32)
    moved, counts = compact(fields[...], LIVE, rows, LANES // 2)
    row = lax.broadcasted_iota(jnp.int32, (FIELDS, LANES), 0)
    asked = jnp.where(row == COUNT, counts, moved).astype(message.dtype)
    message[:, :wide] = q_nope[...]
    message[:, wide : wide + narrow] = q_rope[...]
    message[:, wide + narrow :] = jnp.concatenate(
        [asked, jnp.zeros((rows - FIELDS, LANES), message.dtype)], axis=0
    )
    own[...] = jnp.zeros_like(own)
    mine = [pick(jnp.minimum(k, held - 1)) for k in range(most)]
    own[:, :rows] = stack([*mine, jnp.minimum(length, held * page)], FIELDS)


def project_queries(message, w_uk, queries, heads, latent, narrow):
    rows = message.shape[0]
    nope = w_uk.shape[1]
    tiles = latent // LANES
    low = lax.broadcasted_iota(jnp.int32, (rows, LANES), 1) < LANES // 2
    for h in range(heads):
        lat = jnp.dot(
            message[:, h * nope : (h + 1) * nope], w_uk[h], preferred_element_type=jnp.float32
        )
        for c in range(tiles):
            queries[c, pl.ds(h, rows, stride=heads), :] = lat[:, c * LANES : (c + 1) * LANES]
    for c in range(narrow // LANES):
        pair = lane_tile(message, heads * nope // LANES + c).astype(jnp.float32)
        swapped = pltpu.roll(pair, LANES // 2, 1)
        for h, left, right in ((2 * c, pair, swapped), (2 * c + 1, swapped, pair)):
            at = pl.ds(h, rows, stride=heads)
            queries[tiles, at, :] = jnp.where(low, left, 0.0)
            queries[tiles + 1, at, :] = jnp.where(low, 0.0, right)


def to_table(moved, count, rows, heads, score_row=None):
    whole = moved.astype(jnp.int32)
    request = whole[ROW : ROW + 1, :]
    query_row = jnp.where(request == 0, rows, request - 1) * heads
    blocks = lax.shift_right_logical(
        count[0:1, :].astype(jnp.int32) + (UNROLL - 1), UNROLL.bit_length() - 1
    )
    row = lax.broadcasted_iota(jnp.int32, whole.shape, 0)
    for k, value in ((ROW, query_row), (COUNT, blocks)):
        whole = jnp.where(row == k, jnp.broadcast_to(value, whole.shape), whole)
    extra = query_row if score_row is None else query_row + score_row(whole)
    return jnp.where(row == SCORE_ROW, jnp.broadcast_to(extra, whole.shape), whole)


def rope_lanes(page, heads):
    quarter = page // 4
    lane = lax.broadcasted_iota(jnp.int32, (heads, LEND * page), 1)
    return lane // page * quarter + lax.rem(lane, page) // 4, lax.rem(lane, 4)


def latent_scores(queries, pool, items, heads):
    tiles = queries.shape[0] - 2
    left, rows = [], []
    for start, slots in items:
        at = pl.ds(start, heads)
        left.append(jnp.concatenate([queries[c, at, :] for c in range(tiles)], axis=1))
        rows += [pool[s] for s in slots]
    parts = lax.dot_general(
        jnp.concatenate(left, axis=0).astype(jnp.bfloat16),
        jnp.concatenate(rows, axis=0),
        (((1,), (1,)), ((), ())),
        preferred_element_type=jnp.float32,
    )
    columns = parts.shape[1] // len(items)
    for i in range(len(items)):
        yield parts[i * heads : (i + 1) * heads, i * columns : (i + 1) * columns]


def rope_scores(queries, rope_keys, items, lanes, heads):
    tiles = queries.shape[0] - 2
    left, rows = [], []
    for start, slots in items:
        turned = jnp.concatenate(
            [queries[tiles, pl.ds(start, heads), :], queries[tiles + 1, pl.ds(start, heads), :]],
            axis=0,
        ).astype(jnp.bfloat16)
        none = jnp.zeros_like(turned)
        left.append(jnp.concatenate([turned, none], axis=1))
        left.append(jnp.concatenate([none, turned], axis=1))
        rows += [rope_keys[s] for s in slots]
    parts = lax.dot_general(
        jnp.concatenate(left, axis=0),
        jnp.concatenate(rows, axis=0),
        (((1,), (1,)), ((), ())),
        preferred_element_type=jnp.float32,
    )
    source, which = lanes
    columns = parts.shape[1] // len(items)
    for i in range(len(items)):
        for j in range(4):
            first = (4 * i + j) * heads
            moved = jnp.take_along_axis(
                parts[first : first + heads, :], source + i * columns, axis=1
            )
            found = moved if j == 0 else jnp.where(which == j, moved, found)
        yield found


def fetch_rows(items, plan, sems):
    copies = [
        pltpu.make_async_copy(items.at[k], plan.at[pl.ds(k * LANES, LANES)], sems.at[k])
        for k in range(TABLE_ROWS)
    ]
    for copy in copies:
        copy.start()
    return copies


def read(plan, row, at):
    return plan[row * LANES + at]


def item(plan, at, heads):
    slots = [read(plan, k, at) for k in range(LEND)]
    return pl.multiple_of(read(plan, ROW, at), heads), slots


def score_work(queries, pool, rope_keys, scores, plan, base, heads, scale):
    page = pool.shape[1]
    scores[...] = jnp.full_like(scores, FAR)
    position = lax.broadcasted_iota(jnp.int32, (heads, LEND * page), 1)
    lanes = rope_lanes(page, heads)
    together = LANES // (LEND * (page // 4))

    @pl.loop(0, read(plan, COUNT, base))
    def _(block):
        first_item = base + block * UNROLL
        items = [item(plan, first_item + u, heads) for u in range(UNROLL)]
        ropes = []
        for first in range(0, UNROLL, together):
            ropes += rope_scores(queries, rope_keys, items[first : first + together], lanes, heads)
        for first in range(0, UNROLL, PAIR):
            mains = latent_scores(queries, pool, items[first : first + PAIR], heads)
            for u, main in enumerate(mains, first):
                start = pl.multiple_of(read(plan, SCORE_ROW, first_item + u), heads)
                scores[pl.ds(start, heads), :] = jnp.where(
                    position < read(plan, LIVE, first_item + u), (main + ropes[u]) * scale, FAR
                )


def soften(scores, weights, norm, lse, total_rows):
    pitch = total_rows + (scores.shape[0] % total_rows) // (scores.shape[0] // total_rows)
    units = scores.shape[0] // pitch
    step = 64
    for r in range(0, total_rows, step):
        block = [scores[j * pitch + r : j * pitch + r + step, :] for j in range(units)]
        top = block[0]
        for one in block[1:]:
            top = jnp.maximum(top, one)
        peak = jnp.max(top, axis=-1, keepdims=True)
        total = jnp.zeros((step, LANES), jnp.float32)
        for j in range(units):
            rounded = jnp.exp(block[j] - peak).astype(jnp.bfloat16).astype(jnp.float32)
            weights[j * pitch + r : j * pitch + r + step, :] = rounded
            total = total + rounded
        total = jnp.sum(total, axis=-1, keepdims=True)
        norm[r : r + step, :] = jnp.broadcast_to(1.0 / total, (step, LANES))
        lse[r : r + step, :] = jnp.broadcast_to(peak + jnp.log(total), (step, LANES))


def value_work(pool, weights, context, plan, base, heads, add):
    @pl.loop(0, read(plan, COUNT, base))
    def _(block):
        for first in range(0, UNROLL, PAIR):
            starts, left, values = [], [], []
            for u in range(first, first + PAIR):
                at = base + block * UNROLL + u
                start, slots = item(plan, at, heads)
                starts.append(start)
                mine = weights[pl.ds(pl.multiple_of(read(plan, SCORE_ROW, at), heads), heads), :]
                none = jnp.zeros_like(mine)
                left.append(
                    jnp.concatenate(
                        [mine if k == u - first else none for k in range(PAIR)], axis=1
                    )
                )
                values += [pool[s] for s in slots]
            summed = jnp.dot(
                jnp.concatenate(left, axis=0).astype(jnp.bfloat16),
                jnp.concatenate(values, axis=0),
                preferred_element_type=jnp.float32,
            )
            for k, start in enumerate(starts):
                for c in range(context.shape[0]):
                    part = summed[k * heads : (k + 1) * heads, c * LANES : (c + 1) * LANES]
                    if add:
                        part = part + context[c, pl.ds(start, heads), :]
                    context[c, pl.ds(start, heads), :] = part


def head_outs(context, norm, w_uv, rows, heads):
    width = w_uv.shape[2]
    for h in range(0, heads, 2):
        pair = []
        for k in range(2):
            at = pl.ds(h + k, rows, stride=heads)
            scale = norm[at, :]
            pair.append(
                jnp.concatenate([context[c, at, :] * scale for c in range(context.shape[0])], axis=1)
            )
        both = jnp.dot(
            jnp.concatenate(pair, axis=0).astype(jnp.bfloat16),
            jnp.concatenate([w_uv[h], w_uv[h + 1]], axis=1),
            preferred_element_type=jnp.float32,
        )
        yield h, both[:rows, :width]
        yield h + 1, both[rows:, width:]


def own_scores_kernel(
    own, message, rope_pages, pool, w_uk,
    rope_keys, weights, norm, lse, items,
    queries, scores, spread, fields, plan, plan_sem,
    *, heads, narrow, most,
):
    slots, page, latent = pool.shape
    rows = message.shape[0]
    units = most // LEND
    scale = 1.0 / math.sqrt(w_uk.shape[1] + narrow // heads)
    tokens = LEND * page
    fields[...] = jnp.zeros_like(fields)
    request = lax.broadcasted_iota(jnp.int32, (1, rows), 1)
    for j in range(units):
        live = jnp.clip(own[most : most + 1, :rows] - j * tokens, 0, tokens)
        values = [own[j * LEND + k : j * LEND + k + 1, :rows] for k in range(LEND)]
        values += [request + 1, live, jnp.zeros_like(live), jnp.full_like(live, j)]
        for k, value in enumerate(values):
            fields[k : k + 1, j * rows : (j + 1) * rows] = value.astype(jnp.float32)
    moved, count = compact(fields[...], LIVE, LANES, LANES)
    pitch = (rows + 1) * heads
    items[...] = to_table(moved, count, rows, heads, lambda w: w[SCORE_ROW : SCORE_ROW + 1, :] * pitch)
    table = fetch_rows(items, plan, plan_sem)
    pieces = page // 2
    spacing = pieces + 1
    for c in range(pieces):
        spread[pl.ds(c, slots, stride=spacing), :] = lane_tile(rope_pages, c).astype(jnp.float32)
    for s in range(slots):
        for side in range(2):
            rows_of = spread[pl.ds(s * spacing + side, pieces // 2, stride=2), :]
            rope_keys[s, :, side * LANES : (side + 1) * LANES] = rows_of.astype(jnp.bfloat16)
    project_queries(message, w_uk, queries, heads, latent, narrow)
    for copy in table:
        copy.wait()
    score_work(queries, pool, rope_keys, scores, plan, 0, heads, scale)
    soften(scores, weights, norm, lse, rows * heads)


def own_values_kernel(items, pool, weights, norm, w_uv, outs, context, plan, plan_sem, *, heads):
    rows = outs.shape[0]
    table = fetch_rows(items, plan, plan_sem)
    context[...] = jnp.zeros_like(context)
    for copy in table:
        copy.wait()
    value_work(pool, weights, context, plan, 0, heads, True)
    width = w_uv.shape[2]
    for h, out in head_outs(context, norm, w_uv, rows, heads):
        outs[:, h * width : (h + 1) * width] = out


def serve_kernel(
    message, pool, rope_keys, w_uk, w_uv, back,
    queries, scores, weights, norm, lse, context, items, plan, plan_sem,
    *, narrow, base,
):
    rows = message.shape[0]
    _, _, latent = pool.shape
    heads = w_uk.shape[0]
    scale = 1.0 / math.sqrt(w_uk.shape[1] + narrow // heads)
    asked = message[0:FIELDS, message.shape[1] - LANES :].astype(jnp.float32)
    items[...] = to_table(asked, asked[COUNT : COUNT + 1, :], rows, heads)
    table = fetch_rows(items, plan, plan_sem)
    context[...] = jnp.zeros_like(context)
    project_queries(message, w_uk, queries, heads, latent, narrow)
    for copy in table:
        copy.wait()
    score_work(queries, pool, rope_keys, scores, plan, base, heads, scale)
    soften(scores, weights, norm, lse, rows * heads)
    value_work(pool, weights, context, plan, base, heads, False)
    width = w_uv.shape[2]
    lane = lax.broadcasted_iota(jnp.int32, (rows, LANES), 1)
    logs = jnp.zeros((rows, LANES), jnp.float32)
    for h, out in head_outs(context, norm, w_uv, rows, heads):
        back[:, h * width : (h + 1) * width] = out.astype(jnp.bfloat16)
        logs = jnp.where(lax.rem(lane, heads) == h, lse[pl.ds(h, rows, stride=heads), :], logs)
    packed = jnp.zeros((rows, LANES), jnp.float32)
    for part in range(3):
        piece = logs.astype(jnp.bfloat16).astype(jnp.float32)
        logs = logs - piece
        packed = jnp.where(lane // heads == part, piece, packed)
    back[:, heads * width :] = packed.astype(jnp.bfloat16)


def join_kernel(outs, lse, from_a, from_b, w_o, sent, kept, joined, *, heads):
    rows = outs.shape[0]
    width = outs.shape[1] // heads
    totals = []
    for arrived in (from_a, from_b):
        tile = arrived[:, heads * width :].astype(jnp.float32)
        total = tile + pltpu.roll(tile, LANES - heads, 1) + pltpu.roll(tile, LANES - 2 * heads, 1)
        totals.append(total)
    for h in range(heads):
        at = slice(h * width, (h + 1) * width)
        logs = [lse[pl.ds(h, rows, stride=heads), :]]
        values = [outs[:, at]]
        for arrived, total in zip((from_a, from_b), totals):
            logs.append(jnp.broadcast_to(total[:, h : h + 1], (rows, LANES)))
            values.append(arrived[:, at].astype(jnp.float32))
        peak = jnp.maximum(jnp.maximum(logs[0], logs[1]), logs[2])
        shares = [jnp.exp(one - peak) for one in logs]
        top = shares[0] * values[0] + shares[1] * values[1] + shares[2] * values[2]
        joined[:, at] = (top / (shares[0] + shares[1] + shares[2])).astype(jnp.bfloat16)
    mine = lax.axis_index("tp")
    other = lax.rem(mine + 1, lax.axis_size("tp"))
    cols = sent.shape[1]
    heads_joined = joined[...]
    away = pl.ds(pl.multiple_of(other * cols, cols), cols)
    here = pl.ds(pl.multiple_of(mine * cols, cols), cols)
    sent[...] = jnp.dot(
        heads_joined, w_o[:, away], preferred_element_type=jnp.float32
    ).astype(jnp.bfloat16)
    kept[...] = jnp.dot(heads_joined, w_o[:, here], preferred_element_type=jnp.float32)


def vmem():
    return pl.BlockSpec(memory_space=pltpu.VMEM)


def in_hbm(array):
    return pltpu.with_memory_space_constraint(array, pltpu.HBM)


def call(kernel, out, ins, scratch, limit, cost=None, **sizes):
    return pl.pallas_call(
        functools.partial(kernel, **sizes),
        out_shape=out,
        in_specs=ins,
        out_specs=jax.tree.map(lambda _: vmem(), out),
        scratch_shapes=scratch,
        compiler_params=pltpu.CompilerParams(vmem_limit_bytes=limit * MIB),
        cost_estimate=cost,
    )


def shards(
    q_nope, q_rope, lengths, page_table, lend_counts, latent_pages, rope_pages, w_uk, w_uv, w_o
):
    rows = lengths.shape[0]
    heads, nope, latent = w_uk.shape
    slots, page, _ = latent_pages.shape
    most = page_table.shape[1]
    width = w_uv.shape[2]
    narrow = q_rope.shape[1]
    tiles = latent // LANES
    units = most // LEND
    assert rows * units <= LANES and FIELDS <= rows <= LANES // 2 and page * LEND == LANES
    f32, bf16, i32 = jnp.float32, jnp.bfloat16, jnp.int32
    shape = jax.ShapeDtypeStruct
    sem = pltpu.SemaphoreType.DMA
    stats = (rows * heads, LANES)
    padded = (rows + 1) * heads
    block = pltpu.VMEM((tiles + 2, padded, LANES), f32)
    contexts = pltpu.VMEM((tiles, padded, LANES), f32)
    plan = pltpu.SMEM((TABLE_ROWS * LANES,), i32)

    message, own = call(
        pack_kernel,
        (shape((rows, heads * nope + narrow + LANES), bf16), shape((FIELDS, LANES), i32)),
        [vmem()] * 5,
        [pltpu.VMEM((FIELDS, LANES), f32)],
        4,
        pl.CostEstimate(flops=20 * 10**9, bytes_accessed=64 * MIB, transcendentals=10**7),
        page=page,
    )(*map(in_hbm, (lengths.reshape(1, rows), page_table.T, lend_counts.T, q_nope, q_rope)))
    asked_b = swap(message, "dp", True)
    asked_a = swap(message, "dp", False)

    rope_keys, weights, norm, lse, items = call(
        own_scores_kernel,
        (
            shape((slots, page // 4, 2 * LANES), bf16),
            shape((units * padded, LANES), f32),
            shape(stats, f32),
            shape(stats, f32),
            shape((FIELDS, LANES), i32),
        ),
        [vmem()] * 5,
        [
            block,
            pltpu.VMEM((units * padded, LANES), f32),
            pltpu.VMEM((slots * (page // 2 + 1), LANES), f32),
            pltpu.VMEM((FIELDS, LANES), f32),
            plan,
            sem((TABLE_ROWS,)),
        ],
        24,
        pl.CostEstimate(
            flops=2 * rows * heads * most * page * (latent + LANES),
            bytes_accessed=slots * page * (latent + LANES) * 2,
            transcendentals=rows * heads * most * page,
        ),
        heads=heads,
        narrow=narrow,
        most=most,
    )(own, message, rope_pages, latent_pages, w_uk)

    serve_scratch = [
        block,
        pltpu.VMEM((padded, LANES), f32),
        pltpu.VMEM((padded, LANES), f32),
        pltpu.VMEM(stats, f32),
        pltpu.VMEM(stats, f32),
        contexts,
        pltpu.VMEM((FIELDS, LANES), i32),
        plan,
        sem((TABLE_ROWS,)),
    ]

    def serve(asked, base):
        return call(
            serve_kernel,
            shape((rows, heads * width + LANES), bf16),
            [vmem()] * 5,
            serve_scratch,
            8,
            narrow=narrow,
            base=base,
        )(asked, latent_pages, rope_keys, w_uk, w_uv)

    back_b = serve(asked_b, LANES // 2)
    from_b = swap(back_b, "dp", True)
    back_a = serve(asked_a, 0)
    from_a = swap(back_a, "dp", False)
    outs = call(
        own_values_kernel,
        shape((rows, heads * width), f32),
        [vmem()] * 5,
        [contexts, plan, sem((TABLE_ROWS,))],
        8,
        heads=heads,
    )(items, latent_pages, weights, norm, w_uv)
    cols = w_o.shape[1] // lax.axis_size("tp")
    sent, kept = call(
        join_kernel,
        (shape((rows, cols), bf16), shape((rows, cols), f32)),
        [vmem()] * 5,
        [pltpu.VMEM((rows, heads * width), bf16)],
        8,
        heads=heads,
    )(outs, lse, from_a, from_b, w_o)
    return (kept + swap(sent, "tp", False).astype(f32)).astype(bf16)


def solution(mesh):
    in_specs = (
        P("dp", "tp"),
        P("dp", "tp"),
        P("dp"),
        P("dp", None),
        P("dp", None),
        P("dp", None, None),
        P("dp", None),
        P("tp", None, None),
        P("tp", None, None),
        P("tp", None),
    )
    out_specs = P("dp", "tp")

    return jax.shard_map(shards, mesh=mesh, in_specs=in_specs, out_specs=out_specs, check_vma=False)
```

```python
import functools
import math

import jax
import jax.numpy as jnp
from jax import lax
from jax.experimental import pallas as pl
from jax.experimental.pallas import tpu as pltpu
from jax.sharding import PartitionSpec as P


LEND = 2
LANES = 128
FIELDS = 16
ROW, LIVE, COUNT, SCORE_ROW = 2, 3, 4, 5
TABLE_ROWS = 6
FAR = -1e30
UNROLL = 8
PAIR = 2
MIB = 1 << 20


def swap(block, axis, odd_first):
    count = lax.axis_size(axis)
    shift = 1 if odd_first else 0
    pairs = []
    for start in range(shift, count + shift, 2):
        a, b = start % count, (start + 1) % count
        pairs += [(a, b), (b, a)]
    return lax.ppermute(block, axis, pairs)


def lane_tile(ref, index):
    return ref[:, index * LANES : (index + 1) * LANES]


def compact(fields, live_row, segment, spacing):
    height, lanes = fields.shape
    row = lax.broadcasted_iota(jnp.int32, (lanes, lanes), 0)
    column = lax.broadcasted_iota(jnp.int32, (lanes, lanes), 1)
    kept = jnp.where(fields[live_row : live_row + 1, :] > 0.0, 1.0, 0.0)
    kept = jnp.broadcast_to(kept, (height, lanes))
    ahead = (row // segment == column // segment) & (row < column)
    inside = row // segment == column // spacing
    place = jnp.dot(
        kept.astype(jnp.bfloat16),
        jnp.where(ahead, 1.0, 0.0).astype(jnp.bfloat16),
        preferred_element_type=jnp.float32,
    )
    count = jnp.dot(
        kept.astype(jnp.bfloat16),
        jnp.where(inside, 1.0, 0.0).astype(jnp.bfloat16),
        preferred_element_type=jnp.float32,
    )
    lane = lax.broadcasted_iota(jnp.int32, (height, lanes), 1)
    target = place.astype(jnp.int32) + lane // segment * spacing
    target = jnp.where(kept > 0.0, target, -1)
    chosen = jnp.where(jnp.broadcast_to(target[0:1, :], (lanes, lanes)) == row, 1.0, 0.0)
    moved = lax.dot_general(
        fields.astype(jnp.bfloat16),
        chosen.astype(jnp.bfloat16),
        (((1,), (1,)), ((), ())),
        preferred_element_type=jnp.float32,
    )
    return moved, count


def pack_kernel(lengths, table, lend, q_nope, q_rope, message, own, fields, *, page):
    rows = q_nope.shape[0]
    most = table.shape[0]
    shift = page.bit_length() - 1
    wide, narrow = q_nope.shape[1], q_rope.shape[1]
    length = lengths[...]
    count = lax.shift_right_logical(length + (page - 1), shift)
    to_prev, to_next = lend[0:1, :], lend[1:2, :]
    held = count - to_prev - to_next
    request = lax.broadcasted_iota(jnp.int32, (1, rows), 1)

    def pick(index):
        found = jnp.zeros_like(index)
        for k in range(most):
            found = jnp.where(index == k, table[k : k + 1, :], found)
        return found

    def lent(first, number):
        slots = [pick(jnp.minimum(first + k, count - 1)) for k in range(LEND)]
        live = jnp.minimum(length - first * page, number * page)
        return [*slots, request + 1, jnp.maximum(live, 0)]

    def stack(values, height):
        row = lax.broadcasted_iota(jnp.int32, (height, rows), 0)
        block = jnp.zeros((height, rows), jnp.int32)
        for k, value in enumerate(values):
            block = jnp.where(row == k, jnp.broadcast_to(value, (height, rows)), block)
        return block

    prev, nxt = lent(held, to_prev), lent(count - to_next, to_next)
    odd = lax.rem(lax.axis_index("dp"), 2) == 1
    fields[...] = jnp.zeros_like(fields)
    for k, (yes, no) in enumerate(((prev, nxt), (nxt, prev))):
        mine = stack([jnp.where(odd, p, n) for p, n in zip(yes, no)], FIELDS)
        fields[:, k * rows : (k + 1) * rows] = mine.astype(jnp.float32)
    moved, counts = compact(fields[...], LIVE, rows, LANES // 2)
    row = lax.broadcasted_iota(jnp.int32, (FIELDS, LANES), 0)
    asked = jnp.where(row == COUNT, counts, moved).astype(message.dtype)
    message[:, :wide] = q_nope[...]
    message[:, wide : wide + narrow] = q_rope[...]
    message[:, wide + narrow :] = jnp.concatenate(
        [asked, jnp.zeros((rows - FIELDS, LANES), message.dtype)], axis=0
    )
    own[...] = jnp.zeros_like(own)
    mine = [pick(jnp.minimum(k, held - 1)) for k in range(most)]
    own[:, :rows] = stack([*mine, jnp.minimum(length, held * page)], FIELDS)


def project_queries(message, w_uk, queries, heads, latent, narrow):
    rows = message.shape[0]
    nope = w_uk.shape[1]
    tiles = latent // LANES
    low = lax.broadcasted_iota(jnp.int32, (rows, LANES), 1) < LANES // 2
    for h in range(0, heads, 2):
        first = message[:, h * nope : (h + 1) * nope]
        second = message[:, (h + 1) * nope : (h + 2) * nope]
        none = jnp.zeros_like(first)
        both = jnp.dot(
            jnp.concatenate(
                [
                    jnp.concatenate([first, none], axis=1),
                    jnp.concatenate([none, second], axis=1),
                ],
                axis=0,
            ),
            jnp.concatenate([w_uk[h], w_uk[h + 1]], axis=0),
            preferred_element_type=jnp.float32,
        )
        for k in range(2):
            for c in range(tiles):
                queries[c, pl.ds(h + k, rows, stride=heads), :] = both[
                    k * rows : (k + 1) * rows, c * LANES : (c + 1) * LANES
                ]
    for c in range(narrow // LANES):
        pair = lane_tile(message, heads * nope // LANES + c).astype(jnp.float32)
        swapped = pltpu.roll(pair, LANES // 2, 1)
        for h, left, right in ((2 * c, pair, swapped), (2 * c + 1, swapped, pair)):
            at = pl.ds(h, rows, stride=heads)
            queries[tiles, at, :] = jnp.where(low, left, 0.0)
            queries[tiles + 1, at, :] = jnp.where(low, 0.0, right)


def to_table(moved, count, rows, heads, score_row=None):
    whole = moved.astype(jnp.int32)
    request = whole[ROW : ROW + 1, :]
    query_row = jnp.where(request == 0, rows, request - 1) * heads
    blocks = lax.shift_right_logical(
        count[0:1, :].astype(jnp.int32) + (UNROLL - 1), UNROLL.bit_length() - 1
    )
    row = lax.broadcasted_iota(jnp.int32, whole.shape, 0)
    for k, value in ((ROW, query_row), (COUNT, blocks)):
        whole = jnp.where(row == k, jnp.broadcast_to(value, whole.shape), whole)
    extra = query_row if score_row is None else query_row + score_row(whole)
    return jnp.where(row == SCORE_ROW, jnp.broadcast_to(extra, whole.shape), whole)


def rope_lanes(page, heads):
    quarter = page // 4
    lane = lax.broadcasted_iota(jnp.int32, (heads, LEND * page), 1)
    return lane // page * quarter + lax.rem(lane, page) // 4, lax.rem(lane, 4)


def latent_scores(queries, pool, items, heads):
    tiles = queries.shape[0] - 2
    left, rows = [], []
    for start, slots in items:
        at = pl.ds(start, heads)
        left.append(jnp.concatenate([queries[c, at, :] for c in range(tiles)], axis=1))
        rows += [pool[s] for s in slots]
    parts = lax.dot_general(
        jnp.concatenate(left, axis=0).astype(jnp.bfloat16),
        jnp.concatenate(rows, axis=0),
        (((1,), (1,)), ((), ())),
        preferred_element_type=jnp.float32,
    )
    columns = parts.shape[1] // len(items)
    for i in range(len(items)):
        yield parts[i * heads : (i + 1) * heads, i * columns : (i + 1) * columns]


def rope_scores(queries, rope_keys, items, lanes, heads):
    tiles = queries.shape[0] - 2
    left, rows = [], []
    for start, slots in items:
        turned = jnp.concatenate(
            [queries[tiles, pl.ds(start, heads), :], queries[tiles + 1, pl.ds(start, heads), :]],
            axis=0,
        ).astype(jnp.bfloat16)
        none = jnp.zeros_like(turned)
        left.append(jnp.concatenate([turned, none], axis=1))
        left.append(jnp.concatenate([none, turned], axis=1))
        rows += [rope_keys[s] for s in slots]
    parts = lax.dot_general(
        jnp.concatenate(left, axis=0),
        jnp.concatenate(rows, axis=0),
        (((1,), (1,)), ((), ())),
        preferred_element_type=jnp.float32,
    )
    source, which = lanes
    columns = parts.shape[1] // len(items)
    for i in range(len(items)):
        for j in range(4):
            first = (4 * i + j) * heads
            moved = jnp.take_along_axis(
                parts[first : first + heads, :], source + i * columns, axis=1
            )
            found = moved if j == 0 else jnp.where(which == j, moved, found)
        yield found


def fetch_rows(items, plan, sems):
    copies = [
        pltpu.make_async_copy(items.at[k], plan.at[pl.ds(k * LANES, LANES)], sems.at[k])
        for k in range(TABLE_ROWS)
    ]
    for copy in copies:
        copy.start()
    return copies


def read(plan, row, at):
    return plan[row * LANES + at]


def item(plan, at, heads):
    slots = [read(plan, k, at) for k in range(LEND)]
    return pl.multiple_of(read(plan, ROW, at), heads), slots


def score_work(queries, pool, rope_keys, scores, plan, base, heads, scale):
    page = pool.shape[1]
    scores[...] = jnp.full_like(scores, FAR)
    position = lax.broadcasted_iota(jnp.int32, (heads, LEND * page), 1)
    lanes = rope_lanes(page, heads)
    together = LANES // (LEND * (page // 4))

    @pl.loop(0, read(plan, COUNT, base))
    def _(block):
        first_item = base + block * UNROLL
        items = [item(plan, first_item + u, heads) for u in range(UNROLL)]
        ropes = []
        for first in range(0, UNROLL, together):
            ropes += rope_scores(queries, rope_keys, items[first : first + together], lanes, heads)
        for first in range(0, UNROLL, PAIR):
            mains = latent_scores(queries, pool, items[first : first + PAIR], heads)
            for u, main in enumerate(mains, first):
                start = pl.multiple_of(read(plan, SCORE_ROW, first_item + u), heads)
                scores[pl.ds(start, heads), :] = jnp.where(
                    position < read(plan, LIVE, first_item + u), (main + ropes[u]) * scale, FAR
                )


def soften(scores, weights, norm, lse, total_rows):
    pitch = total_rows + (scores.shape[0] % total_rows) // (scores.shape[0] // total_rows)
    units = scores.shape[0] // pitch
    step = 64
    for r in range(0, total_rows, step):
        block = [scores[j * pitch + r : j * pitch + r + step, :] for j in range(units)]
        top = block[0]
        for one in block[1:]:
            top = jnp.maximum(top, one)
        peak = jnp.max(top, axis=-1, keepdims=True)
        total = jnp.zeros((step, LANES), jnp.float32)
        for j in range(units):
            rounded = jnp.exp(block[j] - peak).astype(jnp.bfloat16).astype(jnp.float32)
            weights[j * pitch + r : j * pitch + r + step, :] = rounded
            total = total + rounded
        total = jnp.sum(total, axis=-1, keepdims=True)
        norm[r : r + step, :] = jnp.broadcast_to(1.0 / total, (step, LANES))
        lse[r : r + step, :] = jnp.broadcast_to(peak + jnp.log(total), (step, LANES))


def value_work(pool, weights, context, plan, base, heads, add):
    @pl.loop(0, read(plan, COUNT, base))
    def _(block):
        for first in range(0, UNROLL, PAIR):
            starts, left, values = [], [], []
            for u in range(first, first + PAIR):
                at = base + block * UNROLL + u
                start, slots = item(plan, at, heads)
                starts.append(start)
                mine = weights[pl.ds(pl.multiple_of(read(plan, SCORE_ROW, at), heads), heads), :]
                none = jnp.zeros_like(mine)
                left.append(
                    jnp.concatenate(
                        [mine if k == u - first else none for k in range(PAIR)], axis=1
                    )
                )
                values += [pool[s] for s in slots]
            summed = jnp.dot(
                jnp.concatenate(left, axis=0).astype(jnp.bfloat16),
                jnp.concatenate(values, axis=0),
                preferred_element_type=jnp.float32,
            )
            for k, start in enumerate(starts):
                for c in range(context.shape[0]):
                    part = summed[k * heads : (k + 1) * heads, c * LANES : (c + 1) * LANES]
                    if add:
                        part = part + context[c, pl.ds(start, heads), :]
                    context[c, pl.ds(start, heads), :] = part


def head_outs(context, norm, w_uv, rows, heads):
    width = w_uv.shape[2]
    for h in range(0, heads, 2):
        pair = []
        for k in range(2):
            at = pl.ds(h + k, rows, stride=heads)
            scale = norm[at, :]
            pair.append(
                jnp.concatenate([context[c, at, :] * scale for c in range(context.shape[0])], axis=1)
            )
        both = jnp.dot(
            jnp.concatenate(pair, axis=0).astype(jnp.bfloat16),
            jnp.concatenate([w_uv[h], w_uv[h + 1]], axis=1),
            preferred_element_type=jnp.float32,
        )
        yield h, both[:rows, :width]
        yield h + 1, both[rows:, width:]


def heads_in_lanes(lse, rows, heads):
    lane = lax.rem(lax.broadcasted_iota(jnp.int32, (rows, LANES), 1), heads)
    logs = jnp.zeros((rows, LANES), jnp.float32)
    for h in range(heads):
        logs = jnp.where(lane == h, lse[pl.ds(h, rows, stride=heads), :], logs)
    return logs


def own_scores_kernel(
    own, message, rope_pages, pool, w_uk,
    rope_keys, weights, norm, lse, items,
    queries, scores, spread, fields, plan, plan_sem,
    *, heads, narrow, most,
):
    slots, page, latent = pool.shape
    rows = message.shape[0]
    units = most // LEND
    scale = 1.0 / math.sqrt(w_uk.shape[1] + narrow // heads)
    tokens = LEND * page
    fields[...] = jnp.zeros_like(fields)
    request = lax.broadcasted_iota(jnp.int32, (1, rows), 1)
    for j in range(units):
        live = jnp.clip(own[most : most + 1, :rows] - j * tokens, 0, tokens)
        values = [own[j * LEND + k : j * LEND + k + 1, :rows] for k in range(LEND)]
        values += [request + 1, live, jnp.zeros_like(live), jnp.full_like(live, j)]
        for k, value in enumerate(values):
            fields[k : k + 1, j * rows : (j + 1) * rows] = value.astype(jnp.float32)
    moved, count = compact(fields[...], LIVE, LANES, LANES)
    pitch = (rows + 1) * heads
    items[...] = to_table(moved, count, rows, heads, lambda w: w[SCORE_ROW : SCORE_ROW + 1, :] * pitch)
    table = fetch_rows(items, plan, plan_sem)
    pieces = page // 2
    spacing = pieces + 1
    for c in range(pieces):
        spread[pl.ds(c, slots, stride=spacing), :] = lane_tile(rope_pages, c).astype(jnp.float32)
    for s in range(slots):
        for side in range(2):
            rows_of = spread[pl.ds(s * spacing + side, pieces // 2, stride=2), :]
            rope_keys[s, :, side * LANES : (side + 1) * LANES] = rows_of.astype(jnp.bfloat16)
    project_queries(message, w_uk, queries, heads, latent, narrow)
    for copy in table:
        copy.wait()
    score_work(queries, pool, rope_keys, scores, plan, 0, heads, scale)
    soften(scores, weights, norm, lse, rows * heads)


def own_values_kernel(
    items, pool, weights, norm, lse, w_uv, outs, logs, context, plan, plan_sem, *, heads
):
    rows = outs.shape[0]
    table = fetch_rows(items, plan, plan_sem)
    context[...] = jnp.zeros_like(context)
    logs[...] = heads_in_lanes(lse, rows, heads)
    for copy in table:
        copy.wait()
    value_work(pool, weights, context, plan, 0, heads, True)
    width = w_uv.shape[2]
    for h, out in head_outs(context, norm, w_uv, rows, heads):
        outs[:, h * width : (h + 1) * width] = out


def serve_kernel(
    message, pool, rope_keys, w_uk, w_uv, back,
    queries, scores, weights, norm, lse, context, items, plan, plan_sem,
    *, narrow, base,
):
    rows = message.shape[0]
    _, _, latent = pool.shape
    heads = w_uk.shape[0]
    scale = 1.0 / math.sqrt(w_uk.shape[1] + narrow // heads)
    asked = message[0:FIELDS, message.shape[1] - LANES :].astype(jnp.float32)
    items[...] = to_table(asked, asked[COUNT : COUNT + 1, :], rows, heads)
    table = fetch_rows(items, plan, plan_sem)
    context[...] = jnp.zeros_like(context)
    project_queries(message, w_uk, queries, heads, latent, narrow)
    for copy in table:
        copy.wait()
    score_work(queries, pool, rope_keys, scores, plan, base, heads, scale)
    soften(scores, weights, norm, lse, rows * heads)
    value_work(pool, weights, context, plan, base, heads, False)
    width = w_uv.shape[2]
    lane = lax.broadcasted_iota(jnp.int32, (rows, LANES), 1)
    for h, out in head_outs(context, norm, w_uv, rows, heads):
        back[:, h * width : (h + 1) * width] = out.astype(jnp.bfloat16)
    logs = heads_in_lanes(lse, rows, heads)
    packed = jnp.zeros((rows, LANES), jnp.float32)
    for part in range(3):
        piece = logs.astype(jnp.bfloat16).astype(jnp.float32)
        logs = logs - piece
        packed = jnp.where(lane // heads == part, piece, packed)
    back[:, heads * width :] = packed.astype(jnp.bfloat16)


def join_kernel(outs, logs, from_a, from_b, w_o, sent, joined, *, heads):
    rows = outs.shape[0]
    width = outs.shape[1] // heads
    logs = [logs[...]]
    for arrived in (from_a, from_b):
        tile = arrived[:, heads * width :].astype(jnp.float32)
        logs.append(
            tile + pltpu.roll(tile, LANES - heads, 1) + pltpu.roll(tile, LANES - 2 * heads, 1)
        )
    peak = jnp.maximum(jnp.maximum(logs[0], logs[1]), logs[2])
    shares = [jnp.exp(one - peak) for one in logs]
    whole = 1.0 / (shares[0] + shares[1] + shares[2])
    shares = [share * whole for share in shares]
    for h in range(heads):
        at = slice(h * width, (h + 1) * width)
        top = 0.0
        for values, share in zip((outs, from_a, from_b), shares):
            mine = jnp.broadcast_to(share[:, h : h + 1], (rows, width))
            top = top + mine * values[:, at].astype(jnp.float32)
        joined[:, at] = top.astype(jnp.bfloat16)
    other = lax.rem(lax.axis_index("tp") + 1, lax.axis_size("tp"))
    project_out(joined, w_o, other, sent)


def project_out(joined, w_o, part, out):
    cols = out.shape[1]
    at = pl.ds(pl.multiple_of(part * cols, cols), cols)
    out[...] = jnp.dot(joined[...], w_o[:, at], preferred_element_type=jnp.float32).astype(out.dtype)


def keep_kernel(joined, w_o, kept):
    project_out(joined, w_o, lax.axis_index("tp"), kept)


def vmem():
    return pl.BlockSpec(memory_space=pltpu.VMEM)


def in_hbm(array):
    return pltpu.with_memory_space_constraint(array, pltpu.HBM)


def call(kernel, out, ins, scratch, limit, cost=None, **sizes):
    return pl.pallas_call(
        functools.partial(kernel, **sizes),
        out_shape=out,
        in_specs=ins,
        out_specs=jax.tree.map(lambda _: vmem(), out),
        scratch_shapes=scratch,
        compiler_params=pltpu.CompilerParams(vmem_limit_bytes=limit * MIB),
        cost_estimate=cost,
    )


def shards(
    q_nope, q_rope, lengths, page_table, lend_counts, latent_pages, rope_pages, w_uk, w_uv, w_o
):
    rows = lengths.shape[0]
    heads, nope, latent = w_uk.shape
    slots, page, _ = latent_pages.shape
    most = page_table.shape[1]
    width = w_uv.shape[2]
    narrow = q_rope.shape[1]
    tiles = latent // LANES
    units = most // LEND
    assert rows * units <= LANES and FIELDS <= rows <= LANES // 2 and page * LEND == LANES
    f32, bf16, i32 = jnp.float32, jnp.bfloat16, jnp.int32
    shape = jax.ShapeDtypeStruct
    sem = pltpu.SemaphoreType.DMA
    stats = (rows * heads, LANES)
    padded = (rows + 1) * heads
    block = pltpu.VMEM((tiles + 2, padded, LANES), f32)
    contexts = pltpu.VMEM((tiles, padded, LANES), f32)
    plan = pltpu.SMEM((TABLE_ROWS * LANES,), i32)

    message, own = call(
        pack_kernel,
        (shape((rows, heads * nope + narrow + LANES), bf16), shape((FIELDS, LANES), i32)),
        [vmem()] * 5,
        [pltpu.VMEM((FIELDS, LANES), f32)],
        4,
        pl.CostEstimate(flops=20 * 10**9, bytes_accessed=64 * MIB, transcendentals=10**7),
        page=page,
    )(*map(in_hbm, (lengths.reshape(1, rows), page_table.T, lend_counts.T, q_nope, q_rope)))
    asked_b = swap(message, "dp", True)
    asked_a = swap(message, "dp", False)

    rope_keys, weights, norm, lse, items = call(
        own_scores_kernel,
        (
            shape((slots, page // 4, 2 * LANES), bf16),
            shape((units * padded, LANES), f32),
            shape(stats, f32),
            shape(stats, f32),
            shape((FIELDS, LANES), i32),
        ),
        [vmem()] * 5,
        [
            block,
            pltpu.VMEM((units * padded, LANES), f32),
            pltpu.VMEM((slots * (page // 2 + 1), LANES), f32),
            pltpu.VMEM((FIELDS, LANES), f32),
            plan,
            sem((TABLE_ROWS,)),
        ],
        24,
        pl.CostEstimate(
            flops=2 * rows * heads * most * page * (latent + LANES),
            bytes_accessed=slots * page * (latent + LANES) * 2,
            transcendentals=rows * heads * most * page,
        ),
        heads=heads,
        narrow=narrow,
        most=most,
    )(own, message, rope_pages, latent_pages, w_uk)

    serve_scratch = [
        block,
        pltpu.VMEM((padded, LANES), f32),
        pltpu.VMEM((padded, LANES), f32),
        pltpu.VMEM(stats, f32),
        pltpu.VMEM(stats, f32),
        contexts,
        pltpu.VMEM((FIELDS, LANES), i32),
        plan,
        sem((TABLE_ROWS,)),
    ]

    def serve(asked, base):
        return call(
            serve_kernel,
            shape((rows, heads * width + LANES), bf16),
            [vmem()] * 5,
            serve_scratch,
            8,
            narrow=narrow,
            base=base,
        )(asked, latent_pages, rope_keys, w_uk, w_uv)

    back_b = serve(asked_b, LANES // 2)
    from_b = swap(back_b, "dp", True)
    back_a = serve(asked_a, 0)
    from_a = swap(back_a, "dp", False)
    outs, logs = call(
        own_values_kernel,
        (shape((rows, heads * width), f32), shape((rows, LANES), f32)),
        [vmem()] * 6,
        [contexts, plan, sem((TABLE_ROWS,))],
        8,
        heads=heads,
    )(items, latent_pages, weights, norm, lse, w_uv)
    cols = w_o.shape[1] // lax.axis_size("tp")
    sent, joined = call(
        join_kernel,
        (shape((rows, cols), bf16), shape((rows, heads * width), bf16)),
        [vmem()] * 5,
        [],
        8,
        heads=heads,
    )(outs, logs, from_a, from_b, w_o)
    arrived = swap(sent, "tp", False)
    kept = call(keep_kernel, shape((rows, cols), f32), [vmem()] * 2, [], 8)(joined, w_o)
    return (kept + arrived.astype(f32)).astype(bf16)


def solution(mesh):
    in_specs = (
        P("dp", "tp"),
        P("dp", "tp"),
        P("dp"),
        P("dp", None),
        P("dp", None),
        P("dp", None, None),
        P("dp", None),
        P("tp", None, None),
        P("tp", None, None),
        P("tp", None),
    )
    out_specs = P("dp", "tp")

    return jax.shard_map(shards, mesh=mesh, in_specs=in_specs, out_specs=out_specs, check_vma=False)
```

```python
import functools
import math

import jax
import jax.numpy as jnp
from jax import lax
from jax.experimental import pallas as pl
from jax.experimental.pallas import tpu as pltpu
from jax.sharding import PartitionSpec as P


LEND = 2
LANES = 128
FIELDS = 16
ROW, LIVE, COUNT, SCORE_ROW = 2, 3, 4, 5
TABLE_ROWS = 6
FAR = -1e30
UNROLL = 8
PAIR = 2
MIB = 1 << 20


def swap(block, axis, odd_first):
    count = lax.axis_size(axis)
    shift = 1 if odd_first else 0
    pairs = []
    for start in range(shift, count + shift, 2):
        a, b = start % count, (start + 1) % count
        pairs += [(a, b), (b, a)]
    return lax.ppermute(block, axis, pairs)


def lane_tile(ref, index):
    return ref[:, index * LANES : (index + 1) * LANES]


def compact(fields, live_row, segment, spacing):
    height, lanes = fields.shape
    row = lax.broadcasted_iota(jnp.int32, (lanes, lanes), 0)
    column = lax.broadcasted_iota(jnp.int32, (lanes, lanes), 1)
    kept = jnp.where(fields[live_row : live_row + 1, :] > 0.0, 1.0, 0.0)
    kept = jnp.broadcast_to(kept, (height, lanes))
    ahead = (row // segment == column // segment) & (row < column)
    inside = row // segment == column // spacing
    place = jnp.dot(
        kept.astype(jnp.bfloat16),
        jnp.where(ahead, 1.0, 0.0).astype(jnp.bfloat16),
        preferred_element_type=jnp.float32,
    )
    count = jnp.dot(
        kept.astype(jnp.bfloat16),
        jnp.where(inside, 1.0, 0.0).astype(jnp.bfloat16),
        preferred_element_type=jnp.float32,
    )
    lane = lax.broadcasted_iota(jnp.int32, (height, lanes), 1)
    target = place.astype(jnp.int32) + lane // segment * spacing
    target = jnp.where(kept > 0.0, target, -1)
    chosen = jnp.where(jnp.broadcast_to(target[0:1, :], (lanes, lanes)) == row, 1.0, 0.0)
    moved = lax.dot_general(
        fields.astype(jnp.bfloat16),
        chosen.astype(jnp.bfloat16),
        (((1,), (1,)), ((), ())),
        preferred_element_type=jnp.float32,
    )
    return moved, count


def pack_kernel(
    lengths_hbm, table_hbm, lend_hbm, q_nope, q_rope,
    message, own,
    lengths, table, lend, fields, sems,
    *, page,
):
    rows = q_nope.shape[0]
    most = table.shape[0]
    shift = page.bit_length() - 1
    wide, narrow = q_nope.shape[1], q_rope.shape[1]
    routes = (
        (lengths_hbm, lengths),
        (table_hbm, table),
        (lend_hbm, lend),
        (q_nope, message.at[:, pl.ds(0, wide)]),
        (q_rope, message.at[:, pl.ds(wide, narrow)]),
    )
    copies = [pltpu.make_async_copy(*route, sems.at[k]) for k, route in enumerate(routes)]
    for copy in copies:
        copy.start()
    for copy in copies[:3]:
        copy.wait()
    length = lengths[...]
    count = lax.shift_right_logical(length + (page - 1), shift)
    to_prev, to_next = lend[0:1, :], lend[1:2, :]
    held = count - to_prev - to_next
    request = lax.broadcasted_iota(jnp.int32, (1, rows), 1)

    def pick(index):
        found = jnp.zeros_like(index)
        for k in range(most):
            found = jnp.where(index == k, table[k : k + 1, :], found)
        return found

    def lent(first, number):
        slots = [pick(jnp.minimum(first + k, count - 1)) for k in range(LEND)]
        live = jnp.minimum(length - first * page, number * page)
        return [*slots, request + 1, jnp.maximum(live, 0)]

    def stack(values, height):
        row = lax.broadcasted_iota(jnp.int32, (height, rows), 0)
        block = jnp.zeros((height, rows), jnp.int32)
        for k, value in enumerate(values):
            block = jnp.where(row == k, jnp.broadcast_to(value, (height, rows)), block)
        return block

    prev, nxt = lent(held, to_prev), lent(count - to_next, to_next)
    odd = lax.rem(lax.axis_index("dp"), 2) == 1
    fields[...] = jnp.zeros_like(fields)
    for k, (yes, no) in enumerate(((prev, nxt), (nxt, prev))):
        mine = stack([jnp.where(odd, p, n) for p, n in zip(yes, no)], FIELDS)
        fields[:, k * rows : (k + 1) * rows] = mine.astype(jnp.float32)
    moved, counts = compact(fields[...], LIVE, rows, LANES // 2)
    row = lax.broadcasted_iota(jnp.int32, (FIELDS, LANES), 0)
    asked = jnp.where(row == COUNT, counts, moved).astype(message.dtype)
    message[:, wide + narrow :] = jnp.concatenate(
        [asked, jnp.zeros((rows - FIELDS, LANES), message.dtype)], axis=0
    )
    own[...] = jnp.zeros_like(own)
    mine = [pick(jnp.minimum(k, held - 1)) for k in range(most)]
    own[:, :rows] = stack([*mine, jnp.minimum(length, held * page)], FIELDS)
    for copy in copies[3:]:
        copy.wait()


def project_queries(message, w_uk, queries, heads, latent, narrow):
    rows = message.shape[0]
    nope = w_uk.shape[1]
    tiles = latent // LANES
    low = lax.broadcasted_iota(jnp.int32, (rows, LANES), 1) < LANES // 2
    for h in range(0, heads, 2):
        first = message[:, h * nope : (h + 1) * nope]
        second = message[:, (h + 1) * nope : (h + 2) * nope]
        none = jnp.zeros_like(first)
        both = jnp.dot(
            jnp.concatenate(
                [
                    jnp.concatenate([first, none], axis=1),
                    jnp.concatenate([none, second], axis=1),
                ],
                axis=0,
            ),
            jnp.concatenate([w_uk[h], w_uk[h + 1]], axis=0),
            preferred_element_type=jnp.float32,
        )
        for k in range(2):
            for c in range(tiles):
                queries[c, pl.ds(h + k, rows, stride=heads + 1), :] = both[
                    k * rows : (k + 1) * rows, c * LANES : (c + 1) * LANES
                ]
    for c in range(narrow // LANES):
        pair = lane_tile(message, heads * nope // LANES + c).astype(jnp.float32)
        swapped = pltpu.roll(pair, LANES // 2, 1)
        for h, left, right in ((2 * c, pair, swapped), (2 * c + 1, swapped, pair)):
            at = pl.ds(h, rows, stride=heads + 1)
            queries[tiles, at, :] = jnp.where(low, left, 0.0)
            queries[tiles + 1, at, :] = jnp.where(low, 0.0, right)


def to_table(moved, count, rows, heads, score_row=None):
    whole = moved.astype(jnp.int32)
    request = whole[ROW : ROW + 1, :]
    query_row = jnp.where(request == 0, rows, request - 1)
    blocks = lax.shift_right_logical(
        count[0:1, :].astype(jnp.int32) + (UNROLL - 1), UNROLL.bit_length() - 1
    )
    row = lax.broadcasted_iota(jnp.int32, whole.shape, 0)
    for k, value in ((ROW, query_row * (heads + 1)), (COUNT, blocks)):
        whole = jnp.where(row == k, jnp.broadcast_to(value, whole.shape), whole)
    extra = query_row * heads if score_row is None else query_row * heads + score_row(whole)
    return jnp.where(row == SCORE_ROW, jnp.broadcast_to(extra, whole.shape), whole)


def rope_lanes(page, heads):
    quarter = page // 4
    lane = lax.broadcasted_iota(jnp.int32, (heads, LEND * page), 1)
    return lane // page * quarter + lax.rem(lane, page) // 4, lax.rem(lane, 4)


def latent_scores(queries, pool, items, heads):
    tiles = queries.shape[0] - 2
    left, rows = [], []
    for start, slots in items:
        at = pl.ds(start, heads)
        left.append(jnp.concatenate([queries[c, at, :] for c in range(tiles)], axis=1))
        rows += [pool[s] for s in slots]
    parts = lax.dot_general(
        jnp.concatenate(left, axis=0).astype(jnp.bfloat16),
        jnp.concatenate(rows, axis=0),
        (((1,), (1,)), ((), ())),
        preferred_element_type=jnp.float32,
    )
    columns = parts.shape[1] // len(items)
    for i in range(len(items)):
        yield parts[i * heads : (i + 1) * heads, i * columns : (i + 1) * columns]


def rope_scores(queries, rope_keys, items, lanes, heads):
    tiles = queries.shape[0] - 2
    left, rows = [], []
    for start, slots in items:
        turned = jnp.concatenate(
            [queries[tiles, pl.ds(start, heads), :], queries[tiles + 1, pl.ds(start, heads), :]],
            axis=0,
        ).astype(jnp.bfloat16)
        none = jnp.zeros_like(turned)
        left.append(jnp.concatenate([turned, none], axis=1))
        left.append(jnp.concatenate([none, turned], axis=1))
        rows += [rope_keys[s] for s in slots]
    parts = lax.dot_general(
        jnp.concatenate(left, axis=0),
        jnp.concatenate(rows, axis=0),
        (((1,), (1,)), ((), ())),
        preferred_element_type=jnp.float32,
    )
    source, which = lanes
    columns = parts.shape[1] // len(items)
    for i in range(len(items)):
        for j in range(4):
            first = (4 * i + j) * heads
            moved = jnp.take_along_axis(
                parts[first : first + heads, :], source + i * columns, axis=1
            )
            found = moved if j == 0 else jnp.where(which == j, moved, found)
        yield found


def fetch_rows(items, plan, sems):
    copies = [
        pltpu.make_async_copy(items.at[k], plan.at[pl.ds(k * LANES, LANES)], sems.at[k])
        for k in range(TABLE_ROWS)
    ]
    for copy in copies:
        copy.start()
    return copies


def from_plan(plan, first):
    return lambda row, u: plan[row * LANES + first + u]


def from_table(items, base):
    table = items[0:8, :]
    return lambda row, u: table[row, base + u]


def each_block(plan, items, copies, base, work):
    done = 0
    if items is not None:
        work(from_table(items, base))
        done = 1
    for copy in copies:
        copy.wait()

    @pl.loop(done, plan[COUNT * LANES + base])
    def _(block):
        work(from_plan(plan, base + block * UNROLL))


def score_work(queries, pool, rope_keys, scores, plan, items, copies, base, heads, scale):
    page = pool.shape[1]
    scores[...] = jnp.full_like(scores, FAR)
    position = lax.broadcasted_iota(jnp.int32, (heads, LEND * page), 1)
    lanes = rope_lanes(page, heads)
    together = LANES // (LEND * (page // 4))

    def work(read):
        todo = [(read(ROW, u), [read(k, u) for k in range(LEND)]) for u in range(UNROLL)]
        for first in range(0, UNROLL, together):
            ropes = list(
                rope_scores(queries, rope_keys, todo[first : first + together], lanes, heads)
            )
            for k in range(first, first + together, PAIR):
                mains = latent_scores(queries, pool, todo[k : k + PAIR], heads)
                for u, main in enumerate(mains, k):
                    start = pl.multiple_of(read(SCORE_ROW, u), heads)
                    scores[pl.ds(start, heads), :] = jnp.where(
                        position < read(LIVE, u), (main + ropes[u - first]) * scale, FAR
                    )

    each_block(plan, items, copies, base, work)


def soften(scores, weights, norm, lse, total_rows):
    pitch = total_rows + (scores.shape[0] % total_rows) // (scores.shape[0] // total_rows)
    units = scores.shape[0] // pitch
    step = 128 if units == 1 else 32
    for r in range(0, total_rows, step):
        block = [scores[j * pitch + r : j * pitch + r + step, :] for j in range(units)]
        top = block[0]
        for one in block[1:]:
            top = jnp.maximum(top, one)
        peak = jnp.max(top, axis=-1, keepdims=True)
        total = jnp.zeros((step, LANES), jnp.float32)
        for j in range(units):
            rounded = jnp.exp(block[j] - peak).astype(jnp.bfloat16).astype(jnp.float32)
            weights[j * pitch + r : j * pitch + r + step, :] = rounded
            total = total + rounded
        total = jnp.sum(total, axis=-1, keepdims=True)
        scale = jnp.where(peak > FAR / 2, 1.0 / total, 0.0)
        norm[r : r + step, :] = jnp.broadcast_to(scale, (step, LANES))
        lse[r : r + step, :] = jnp.broadcast_to(peak + jnp.log(total), (step, LANES))


def value_work(pool, weights, context, plan, items, copies, base, heads, add):
    def work(read):
        for first in range(0, UNROLL, PAIR):
            starts, left, values = [], [], []
            for u in range(first, first + PAIR):
                starts.append(read(ROW, u))
                mine = weights[pl.ds(pl.multiple_of(read(SCORE_ROW, u), heads), heads), :]
                none = jnp.zeros_like(mine)
                left.append(
                    jnp.concatenate(
                        [mine if k == u - first else none for k in range(PAIR)], axis=1
                    )
                )
                values += [pool[read(k, u)] for k in range(LEND)]
            summed = jnp.dot(
                jnp.concatenate(left, axis=0).astype(jnp.bfloat16),
                jnp.concatenate(values, axis=0),
                preferred_element_type=jnp.float32,
            )
            for k, start in enumerate(starts):
                for c in range(context.shape[0]):
                    part = summed[k * heads : (k + 1) * heads, c * LANES : (c + 1) * LANES]
                    if add:
                        part = part + context[c, pl.ds(start, heads), :]
                    context[c, pl.ds(start, heads), :] = part

    each_block(plan, items, copies, base, work)


def head_outs(context, norm, w_uv, rows, heads):
    width = w_uv.shape[2]
    for h in range(0, heads, 2):
        pair = []
        for k in range(2):
            scale = norm[pl.ds(h + k, rows, stride=heads), :]
            at = pl.ds(h + k, rows, stride=heads + 1)
            pair.append(
                jnp.concatenate(
                    [
                        jnp.where(scale > 0.0, context[c, at, :] * scale, 0.0)
                        for c in range(context.shape[0])
                    ],
                    axis=1,
                )
            )
        both = jnp.dot(
            jnp.concatenate(pair, axis=0).astype(jnp.bfloat16),
            jnp.concatenate([w_uv[h], w_uv[h + 1]], axis=1),
            preferred_element_type=jnp.float32,
        )
        yield h, both[:rows, :width]
        yield h + 1, both[rows:, width:]


def heads_in_lanes(lse, rows, heads):
    lane = lax.rem(lax.broadcasted_iota(jnp.int32, (rows, LANES), 1), heads)
    logs = jnp.zeros((rows, LANES), jnp.float32)
    for h in range(heads):
        logs = jnp.where(lane == h, lse[pl.ds(h, rows, stride=heads), :], logs)
    return logs


def own_scores_kernel(
    own, message, rope_pages, pool, w_uk,
    rope_keys, weights, norm, lse, items,
    queries, scores, spread, fields, plan, plan_sem,
    *, heads, narrow, most,
):
    slots, page, latent = pool.shape
    rows = message.shape[0]
    units = most // LEND
    scale = 1.0 / math.sqrt(w_uk.shape[1] + narrow // heads)
    tokens = LEND * page
    fields[...] = jnp.zeros_like(fields)
    request = lax.broadcasted_iota(jnp.int32, (1, rows), 1)
    for j in range(units):
        live = jnp.clip(own[most : most + 1, :rows] - j * tokens, 0, tokens)
        values = [own[j * LEND + k : j * LEND + k + 1, :rows] for k in range(LEND)]
        values += [request + 1, live, jnp.zeros_like(live), jnp.full_like(live, j)]
        for k, value in enumerate(values):
            fields[k : k + 1, j * rows : (j + 1) * rows] = value.astype(jnp.float32)
    moved, count = compact(fields[...], LIVE, LANES, LANES)
    pitch = (rows + 1) * heads
    items[...] = to_table(moved, count, rows, heads, lambda w: w[SCORE_ROW : SCORE_ROW + 1, :] * pitch)
    table = fetch_rows(items, plan, plan_sem)
    pieces = page // 2
    spacing = pieces + 1
    for c in range(pieces):
        spread[pl.ds(c, slots, stride=spacing), :] = lane_tile(rope_pages, c).astype(jnp.float32)
    for s in range(slots):
        for side in range(2):
            rows_of = spread[pl.ds(s * spacing + side, pieces // 2, stride=2), :]
            rope_keys[s, :, side * LANES : (side + 1) * LANES] = rows_of.astype(jnp.bfloat16)
    project_queries(message, w_uk, queries, heads, latent, narrow)
    score_work(queries, pool, rope_keys, scores, plan, None, table, 0, heads, scale)
    soften(scores, weights, norm, lse, rows * heads)


def own_values_kernel(
    items, pool, weights, norm, lse, w_uv, outs, logs, context, plan, plan_sem, *, heads
):
    rows = outs.shape[0]
    table = fetch_rows(items, plan, plan_sem)
    context[...] = jnp.zeros_like(context)
    logs[...] = heads_in_lanes(lse, rows, heads)
    value_work(pool, weights, context, plan, items, table, 0, heads, True)
    width = w_uv.shape[2]
    for h, out in head_outs(context, norm, w_uv, rows, heads):
        outs[:, h * width : (h + 1) * width] = out


def serve_kernel(
    message, pool, rope_keys, w_uk, w_uv, back,
    queries, scores, weights, norm, lse, context, items, plan, plan_sem,
    *, narrow, base,
):
    rows = message.shape[0]
    _, _, latent = pool.shape
    heads = w_uk.shape[0]
    scale = 1.0 / math.sqrt(w_uk.shape[1] + narrow // heads)
    asked = message[0:FIELDS, message.shape[1] - LANES :].astype(jnp.float32)
    items[...] = to_table(asked, asked[COUNT : COUNT + 1, :], rows, heads)
    table = fetch_rows(items, plan, plan_sem)
    project_queries(message, w_uk, queries, heads, latent, narrow)
    score_work(queries, pool, rope_keys, scores, plan, items, table, base, heads, scale)
    soften(scores, weights, norm, lse, rows * heads)
    value_work(pool, weights, context, plan, None, (), base, heads, False)
    width = w_uv.shape[2]
    lane = lax.broadcasted_iota(jnp.int32, (rows, LANES), 1)
    for h, out in head_outs(context, norm, w_uv, rows, heads):
        back[:, h * width : (h + 1) * width] = out.astype(jnp.bfloat16)
    logs = heads_in_lanes(lse, rows, heads)
    packed = jnp.zeros((rows, LANES), jnp.float32)
    for part in range(3):
        piece = logs.astype(jnp.bfloat16).astype(jnp.float32)
        logs = logs - piece
        packed = jnp.where(lane // heads == part, piece, packed)
    back[:, heads * width :] = packed.astype(jnp.bfloat16)


def join_kernel(outs, logs, from_a, from_b, w_o, sent, joined, *, heads):
    rows = outs.shape[0]
    width = outs.shape[1] // heads
    logs = [logs[...]]
    for arrived in (from_a, from_b):
        tile = arrived[:, heads * width :].astype(jnp.float32)
        logs.append(
            tile + pltpu.roll(tile, LANES - heads, 1) + pltpu.roll(tile, LANES - 2 * heads, 1)
        )
    peak = jnp.maximum(jnp.maximum(logs[0], logs[1]), logs[2])
    shares = [jnp.exp(one - peak) for one in logs]
    whole = 1.0 / (shares[0] + shares[1] + shares[2])
    shares = [share * whole for share in shares]
    for h in range(heads):
        at = slice(h * width, (h + 1) * width)
        top = 0.0
        for values, share in zip((outs, from_a, from_b), shares):
            mine = jnp.broadcast_to(share[:, h : h + 1], (rows, width))
            top = top + mine * values[:, at].astype(jnp.float32)
        joined[:, at] = top.astype(jnp.bfloat16)
    other = lax.rem(lax.axis_index("tp") + 1, lax.axis_size("tp"))
    project_out(joined, w_o, other, sent)


def project_out(joined, w_o, part, out):
    cols = out.shape[1]
    at = pl.ds(pl.multiple_of(part * cols, cols), cols)
    out[...] = jnp.dot(joined[...], w_o[:, at], preferred_element_type=jnp.float32).astype(out.dtype)


def keep_kernel(joined, w_o, kept):
    project_out(joined, w_o, lax.axis_index("tp"), kept)


def vmem():
    return pl.BlockSpec(memory_space=pltpu.VMEM)


def in_hbm(array):
    return pltpu.with_memory_space_constraint(array, pltpu.HBM)


def call(kernel, out, ins, scratch, limit, cost=None, **sizes):
    return pl.pallas_call(
        functools.partial(kernel, **sizes),
        out_shape=out,
        in_specs=ins,
        out_specs=jax.tree.map(lambda _: vmem(), out),
        scratch_shapes=scratch,
        compiler_params=pltpu.CompilerParams(vmem_limit_bytes=limit * MIB),
        cost_estimate=cost,
    )


def shards(
    q_nope, q_rope, lengths, page_table, lend_counts, latent_pages, rope_pages, w_uk, w_uv, w_o
):
    rows = lengths.shape[0]
    heads, nope, latent = w_uk.shape
    slots, page, _ = latent_pages.shape
    most = page_table.shape[1]
    width = w_uv.shape[2]
    narrow = q_rope.shape[1]
    tiles = latent // LANES
    units = most // LEND
    assert rows * units <= LANES and FIELDS <= rows <= LANES // 2 and page * LEND == LANES
    f32, bf16, i32 = jnp.float32, jnp.bfloat16, jnp.int32
    shape = jax.ShapeDtypeStruct
    sem = pltpu.SemaphoreType.DMA
    stats = (rows * heads, LANES)
    padded = (rows + 1) * heads
    pitched = -(-(rows + 1) * (heads + 1) // 8) * 8
    block = pltpu.VMEM((tiles + 2, pitched, LANES), f32)
    contexts = pltpu.VMEM((tiles, pitched, LANES), f32)
    plan = pltpu.SMEM((TABLE_ROWS * LANES,), i32)

    message, own = call(
        pack_kernel,
        (shape((rows, heads * nope + narrow + LANES), bf16), shape((FIELDS, LANES), i32)),
        [pl.BlockSpec(memory_space=pl.ANY)] * 5,
        [
            pltpu.VMEM((1, rows), i32),
            pltpu.VMEM((most, rows), i32),
            pltpu.VMEM((2, rows), i32),
            pltpu.VMEM((FIELDS, LANES), f32),
            sem((5,)),
        ],
        4,
        pl.CostEstimate(flops=20 * 10**9, bytes_accessed=64 * MIB, transcendentals=10**7),
        page=page,
    )(*map(in_hbm, (lengths.reshape(1, rows), page_table.T, lend_counts.T, q_nope, q_rope)))
    asked_b = swap(message, "dp", True)
    asked_a = swap(message, "dp", False)

    rope_keys, weights, norm, lse, items = call(
        own_scores_kernel,
        (
            shape((slots, page // 4, 2 * LANES), bf16),
            shape((units * padded, LANES), f32),
            shape(stats, f32),
            shape(stats, f32),
            shape((FIELDS, LANES), i32),
        ),
        [vmem()] * 5,
        [
            block,
            pltpu.VMEM((units * padded, LANES), f32),
            pltpu.VMEM((slots * (page // 2 + 1), LANES), f32),
            pltpu.VMEM((FIELDS, LANES), f32),
            plan,
            sem((TABLE_ROWS,)),
        ],
        24,
        pl.CostEstimate(
            flops=2 * rows * heads * most * page * (latent + LANES),
            bytes_accessed=slots * page * (latent + LANES) * 2,
            transcendentals=rows * heads * most * page,
        ),
        heads=heads,
        narrow=narrow,
        most=most,
    )(own, message, rope_pages, latent_pages, w_uk)

    serve_scratch = [
        block,
        pltpu.VMEM((padded, LANES), f32),
        pltpu.VMEM((padded, LANES), f32),
        pltpu.VMEM(stats, f32),
        pltpu.VMEM(stats, f32),
        contexts,
        pltpu.VMEM((FIELDS, LANES), i32),
        plan,
        sem((TABLE_ROWS,)),
    ]

    def serve(asked, base):
        return call(
            serve_kernel,
            shape((rows, heads * width + LANES), bf16),
            [vmem()] * 5,
            serve_scratch,
            8,
            narrow=narrow,
            base=base,
        )(asked, latent_pages, rope_keys, w_uk, w_uv)

    back_b = serve(asked_b, LANES // 2)
    from_b = swap(back_b, "dp", True)
    back_a = serve(asked_a, 0)
    from_a = swap(back_a, "dp", False)
    outs, logs = call(
        own_values_kernel,
        (shape((rows, heads * width), f32), shape((rows, LANES), f32)),
        [vmem()] * 6,
        [contexts, plan, sem((TABLE_ROWS,))],
        8,
        heads=heads,
    )(items, latent_pages, weights, norm, lse, w_uv)
    cols = w_o.shape[1] // lax.axis_size("tp")
    sent, joined = call(
        join_kernel,
        (shape((rows, cols), bf16), shape((rows, heads * width), bf16)),
        [vmem()] * 5,
        [],
        8,
        heads=heads,
    )(outs, logs, from_a, from_b, w_o)
    arrived = swap(sent, "tp", False)
    kept = call(keep_kernel, shape((rows, cols), f32), [vmem()] * 2, [], 8)(joined, w_o)
    return (kept + arrived.astype(f32)).astype(bf16)


def solution(mesh):
    in_specs = (
        P("dp", "tp"),
        P("dp", "tp"),
        P("dp"),
        P("dp", None),
        P("dp", None),
        P("dp", None, None),
        P("dp", None),
        P("tp", None, None),
        P("tp", None, None),
        P("tp", None),
    )
    out_specs = P("dp", "tp")

    return jax.shard_map(shards, mesh=mesh, in_specs=in_specs, out_specs=out_specs, check_vma=False)
```

```python
import functools
import math

import jax
import jax.numpy as jnp
from jax import lax
from jax.experimental import pallas as pl
from jax.experimental.pallas import tpu as pltpu
from jax.sharding import PartitionSpec as P


LEND = 2
LANES = 128
FIELDS = 16
ROW, LIVE, COUNT, SCORE_ROW = 2, 3, 4, 5
TABLE_ROWS = 6
FAR = -1e30
UNROLL = 16
PAIR = 2
QUAD = 1
MIB = 1 << 20


def swap(block, axis, odd_first):
    count = lax.axis_size(axis)
    shift = 1 if odd_first else 0
    pairs = []
    for start in range(shift, count + shift, 2):
        a, b = start % count, (start + 1) % count
        pairs += [(a, b), (b, a)]
    return lax.ppermute(block, axis, pairs)


def lane_tile(ref, index):
    return ref[:, index * LANES : (index + 1) * LANES]


def compact(fields, live_row, segment, spacing):
    height, lanes = fields.shape
    row = lax.broadcasted_iota(jnp.int32, (lanes, lanes), 0)
    column = lax.broadcasted_iota(jnp.int32, (lanes, lanes), 1)
    kept = jnp.where(fields[live_row : live_row + 1, :] > 0.0, 1.0, 0.0)
    kept = jnp.broadcast_to(kept, (height, lanes))
    ahead = (row // segment == column // segment) & (row < column)
    inside = row // segment == column // spacing
    place = jnp.dot(
        kept.astype(jnp.bfloat16),
        jnp.where(ahead, 1.0, 0.0).astype(jnp.bfloat16),
        preferred_element_type=jnp.float32,
    )
    count = jnp.dot(
        kept.astype(jnp.bfloat16),
        jnp.where(inside, 1.0, 0.0).astype(jnp.bfloat16),
        preferred_element_type=jnp.float32,
    )
    lane = lax.broadcasted_iota(jnp.int32, (height, lanes), 1)
    target = place.astype(jnp.int32) + lane // segment * spacing
    target = jnp.where(kept > 0.0, target, -1)
    chosen = jnp.where(jnp.broadcast_to(target[0:1, :], (lanes, lanes)) == row, 1.0, 0.0)
    moved = lax.dot_general(
        fields.astype(jnp.bfloat16),
        chosen.astype(jnp.bfloat16),
        (((1,), (1,)), ((), ())),
        preferred_element_type=jnp.float32,
    )
    return moved, count


def pack_kernel(
    lengths_hbm, table_hbm, lend_hbm, q_nope, q_rope,
    message, own,
    lengths, table, lend, fields, sems,
    *, page,
):
    rows = q_nope.shape[0]
    most = table.shape[0]
    shift = page.bit_length() - 1
    wide, narrow = q_nope.shape[1], q_rope.shape[1]
    routes = (
        (lengths_hbm, lengths),
        (table_hbm, table),
        (lend_hbm, lend),
        (q_nope, message.at[:, pl.ds(0, wide)]),
        (q_rope, message.at[:, pl.ds(wide, narrow)]),
    )
    copies = [pltpu.make_async_copy(*route, sems.at[k]) for k, route in enumerate(routes)]
    for copy in copies:
        copy.start()
    for copy in copies[:3]:
        copy.wait()
    length = lengths[...]
    count = lax.shift_right_logical(length + (page - 1), shift)
    to_prev, to_next = lend[0:1, :], lend[1:2, :]
    held = count - to_prev - to_next
    request = lax.broadcasted_iota(jnp.int32, (1, rows), 1)

    def pick(index):
        found = jnp.zeros_like(index)
        for k in range(most):
            found = jnp.where(index == k, table[k : k + 1, :], found)
        return found

    def lent(first, number):
        slots = [pick(jnp.minimum(first + k, count - 1)) for k in range(LEND)]
        live = jnp.minimum(length - first * page, number * page)
        return [*slots, request + 1, jnp.maximum(live, 0)]

    def stack(values, height):
        row = lax.broadcasted_iota(jnp.int32, (height, rows), 0)
        block = jnp.zeros((height, rows), jnp.int32)
        for k, value in enumerate(values):
            block = jnp.where(row == k, jnp.broadcast_to(value, (height, rows)), block)
        return block

    prev, nxt = lent(held, to_prev), lent(count - to_next, to_next)
    odd = lax.rem(lax.axis_index("dp"), 2) == 1
    fields[...] = jnp.zeros_like(fields)
    for k, (yes, no) in enumerate(((prev, nxt), (nxt, prev))):
        mine = stack([jnp.where(odd, p, n) for p, n in zip(yes, no)], FIELDS)
        fields[:, k * rows : (k + 1) * rows] = mine.astype(jnp.float32)
    moved, counts = compact(fields[...], LIVE, rows, LANES // 2)
    row = lax.broadcasted_iota(jnp.int32, (FIELDS, LANES), 0)
    asked = jnp.where(row == COUNT, counts, moved).astype(message.dtype)
    message[:, wide + narrow :] = jnp.concatenate(
        [asked, jnp.zeros((rows - FIELDS, LANES), message.dtype)], axis=0
    )
    own[...] = jnp.zeros_like(own)
    mine = [pick(jnp.minimum(k, held - 1)) for k in range(most)]
    own[:, :rows] = stack([*mine, jnp.minimum(length, held * page)], FIELDS)
    for copy in copies[3:]:
        copy.wait()


def project_queries(message, w_uk, queries, heads, latent, narrow):
    rows = message.shape[0]
    nope = w_uk.shape[1]
    tiles = latent // LANES
    low = lax.broadcasted_iota(jnp.int32, (rows, LANES), 1) < LANES // 2
    for h in range(0, heads, 2):
        first = message[:, h * nope : (h + 1) * nope]
        second = message[:, (h + 1) * nope : (h + 2) * nope]
        none = jnp.zeros_like(first)
        both = jnp.dot(
            jnp.concatenate(
                [
                    jnp.concatenate([first, none], axis=1),
                    jnp.concatenate([none, second], axis=1),
                ],
                axis=0,
            ),
            jnp.concatenate([w_uk[h], w_uk[h + 1]], axis=0),
            preferred_element_type=jnp.float32,
        )
        for k in range(2):
            for c in range(tiles):
                queries[c, pl.ds(h + k, rows, stride=heads + 1), :] = both[
                    k * rows : (k + 1) * rows, c * LANES : (c + 1) * LANES
                ]
    for c in range(narrow // LANES):
        pair = lane_tile(message, heads * nope // LANES + c).astype(jnp.float32)
        swapped = pltpu.roll(pair, LANES // 2, 1)
        for h, left, right in ((2 * c, pair, swapped), (2 * c + 1, swapped, pair)):
            at = pl.ds(h, rows, stride=heads + 1)
            queries[tiles, at, :] = jnp.where(low, left, 0.0)
            queries[tiles + 1, at, :] = jnp.where(low, 0.0, right)


def to_table(moved, count, rows, heads, score_row=None):
    whole = moved.astype(jnp.int32)
    request = whole[ROW : ROW + 1, :]
    query_row = jnp.where(request == 0, rows, request - 1)
    blocks = lax.shift_right_logical(
        count[0:1, :].astype(jnp.int32) + (UNROLL - 1), UNROLL.bit_length() - 1
    )
    row = lax.broadcasted_iota(jnp.int32, whole.shape, 0)
    for k, value in ((ROW, query_row * (heads + 1)), (COUNT, blocks)):
        whole = jnp.where(row == k, jnp.broadcast_to(value, whole.shape), whole)
    extra = query_row * heads if score_row is None else query_row * heads + score_row(whole)
    return jnp.where(row == SCORE_ROW, jnp.broadcast_to(extra, whole.shape), whole)


def rope_lanes(page, heads):
    quarter = page // 4
    lane = lax.broadcasted_iota(jnp.int32, (heads, LEND * page), 1)
    return lane // page * quarter + lax.rem(lane, page) // 4, lax.rem(lane, 4)


def latent_scores(queries, pool, items, heads):
    tiles = queries.shape[0] - 2
    left, rows = [], []
    for start, slots in items:
        at = pl.ds(start, heads)
        left.append(jnp.concatenate([queries[c, at, :] for c in range(tiles)], axis=1))
        rows += [pool[s] for s in slots]
    parts = lax.dot_general(
        jnp.concatenate(left, axis=0).astype(jnp.bfloat16),
        jnp.concatenate(rows, axis=0),
        (((1,), (1,)), ((), ())),
        preferred_element_type=jnp.float32,
    )
    columns = parts.shape[1] // len(items)
    for i in range(len(items)):
        yield parts[i * heads : (i + 1) * heads, i * columns : (i + 1) * columns]


def rope_scores(queries, rope_keys, items, lanes, heads):
    tiles = queries.shape[0] - 2
    left, rows = [], []
    for start, slots in items:
        turned = jnp.concatenate(
            [queries[tiles, pl.ds(start, heads), :], queries[tiles + 1, pl.ds(start, heads), :]],
            axis=0,
        ).astype(jnp.bfloat16)
        none = jnp.zeros_like(turned)
        left.append(jnp.concatenate([turned, none], axis=1))
        left.append(jnp.concatenate([none, turned], axis=1))
        rows += [rope_keys[s] for s in slots]
    parts = lax.dot_general(
        jnp.concatenate(left, axis=0),
        jnp.concatenate(rows, axis=0),
        (((1,), (1,)), ((), ())),
        preferred_element_type=jnp.float32,
    )
    source, which = lanes
    columns = parts.shape[1] // len(items)
    for i in range(len(items)):
        for j in range(4):
            first = (4 * i + j) * heads
            moved = jnp.take_along_axis(
                parts[first : first + heads, :], source + i * columns, axis=1
            )
            found = moved if j == 0 else jnp.where(which == j, moved, found)
        yield found


def fetch_rows(items, plan, sems):
    copies = [
        pltpu.make_async_copy(items.at[k], plan.at[pl.ds(k * LANES, LANES)], sems.at[k])
        for k in range(TABLE_ROWS)
    ]
    for copy in copies:
        copy.start()
    return copies


def from_plan(plan, first):
    return lambda row, u: plan[row * LANES + first + u]


def from_table(items, base):
    table = items[0:8, :]
    return lambda row, u: table[row, base + u]


def each_block(plan, items, copies, base, work):
    done = 0
    if items is not None:
        work(from_table(items, base))
        done = 1
    for copy in copies:
        copy.wait()

    @pl.loop(done, plan[COUNT * LANES + base])
    def _(block):
        work(from_plan(plan, base + block * UNROLL))


def score_work(queries, pool, rope_keys, scores, plan, items, copies, base, heads, scale):
    page = pool.shape[1]
    scores[...] = jnp.full_like(scores, FAR)
    position = lax.broadcasted_iota(jnp.int32, (heads, LEND * page), 1)
    lanes = rope_lanes(page, heads)
    together = LANES // (LEND * (page // 4))

    def work(read):
        todo = [(read(ROW, u), [read(k, u) for k in range(LEND)]) for u in range(UNROLL)]
        for first in range(0, UNROLL, together):
            ropes = list(
                rope_scores(queries, rope_keys, todo[first : first + together], lanes, heads)
            )
            for k in range(first, first + together, PAIR):
                mains = latent_scores(queries, pool, todo[k : k + PAIR], heads)
                for u, main in enumerate(mains, k):
                    start = pl.multiple_of(read(SCORE_ROW, u), heads)
                    scores[pl.ds(start, heads), :] = jnp.where(
                        position < read(LIVE, u), (main + ropes[u - first]) * scale, FAR
                    )

    each_block(plan, items, copies, base, work)


def soften(scores, weights, norm, lse, total_rows):
    pitch = total_rows + (scores.shape[0] % total_rows) // (scores.shape[0] // total_rows)
    units = scores.shape[0] // pitch
    step = 128 if units == 1 else 32
    for r in range(0, total_rows, step):
        block = [scores[j * pitch + r : j * pitch + r + step, :] for j in range(units)]
        top = block[0]
        for one in block[1:]:
            top = jnp.maximum(top, one)
        peak = jnp.max(top, axis=-1, keepdims=True)
        total = jnp.zeros((step, LANES), jnp.float32)
        for j in range(units):
            rounded = jnp.exp(block[j] - peak).astype(jnp.bfloat16).astype(jnp.float32)
            weights[j * pitch + r : j * pitch + r + step, :] = rounded
            total = total + rounded
        total = jnp.sum(total, axis=-1, keepdims=True)
        scale = jnp.where(peak > FAR / 2, 1.0 / total, 0.0)
        norm[r : r + step, :] = jnp.broadcast_to(scale, (step, LANES))
        lse[r : r + step, :] = jnp.broadcast_to(peak + jnp.log(total), (step, LANES))


def value_work(pool, weights, context, plan, items, copies, base, heads, add):
    def work(read):
        for first in range(0, UNROLL, PAIR):
            starts, left, values = [], [], []
            for u in range(first, first + PAIR):
                starts.append(read(ROW, u))
                mine = weights[pl.ds(pl.multiple_of(read(SCORE_ROW, u), heads), heads), :]
                none = jnp.zeros_like(mine)
                left.append(
                    jnp.concatenate(
                        [mine if k == u - first else none for k in range(PAIR)], axis=1
                    )
                )
                values += [pool[read(k, u)] for k in range(LEND)]
            summed = jnp.dot(
                jnp.concatenate(left, axis=0).astype(jnp.bfloat16),
                jnp.concatenate(values, axis=0),
                preferred_element_type=jnp.float32,
            )
            for k, start in enumerate(starts):
                for c in range(context.shape[0]):
                    part = summed[k * heads : (k + 1) * heads, c * LANES : (c + 1) * LANES]
                    if add:
                        part = part + context[c, pl.ds(start, heads), :]
                    context[c, pl.ds(start, heads), :] = part

    each_block(plan, items, copies, base, work)


def head_outs(context, norm, w_uv, rows, heads):
    width = w_uv.shape[2]
    for first in range(0, heads, QUAD):
        left = []
        for h in range(first, first + QUAD):
            scale = norm[pl.ds(h, rows, stride=heads), :]
            at = pl.ds(h, rows, stride=heads + 1)
            left.append(
                jnp.concatenate(
                    [
                        jnp.where(scale > 0.0, context[c, at, :] * scale, 0.0)
                        for c in range(context.shape[0])
                    ],
                    axis=1,
                )
            )
        found = jnp.dot(
            jnp.concatenate(left, axis=0).astype(jnp.bfloat16),
            jnp.concatenate([w_uv[h] for h in range(first, first + QUAD)], axis=1),
            preferred_element_type=jnp.float32,
        )
        for k in range(QUAD):
            yield first + k, found[k * rows : (k + 1) * rows, k * width : (k + 1) * width]


def heads_in_lanes(lse, rows, heads):
    lane = lax.rem(lax.broadcasted_iota(jnp.int32, (rows, LANES), 1), heads)
    logs = jnp.zeros((rows, LANES), jnp.float32)
    for h in range(heads):
        logs = jnp.where(lane == h, lse[pl.ds(h, rows, stride=heads), :], logs)
    return logs


def own_scores_kernel(
    own, message, rope_pages, pool, w_uk,
    rope_keys, weights, norm, lse, items,
    queries, scores, spread, fields, plan, plan_sem,
    *, heads, narrow, most,
):
    slots, page, latent = pool.shape
    rows = message.shape[0]
    units = most // LEND
    scale = 1.0 / math.sqrt(w_uk.shape[1] + narrow // heads)
    tokens = LEND * page
    fields[...] = jnp.zeros_like(fields)
    request = lax.broadcasted_iota(jnp.int32, (1, rows), 1)
    for j in range(units):
        live = jnp.clip(own[most : most + 1, :rows] - j * tokens, 0, tokens)
        values = [own[j * LEND + k : j * LEND + k + 1, :rows] for k in range(LEND)]
        values += [request + 1, live, jnp.zeros_like(live), jnp.full_like(live, j)]
        for k, value in enumerate(values):
            fields[k : k + 1, j * rows : (j + 1) * rows] = value.astype(jnp.float32)
    moved, count = compact(fields[...], LIVE, LANES, LANES)
    pitch = (rows + 1) * heads
    items[...] = to_table(moved, count, rows, heads, lambda w: w[SCORE_ROW : SCORE_ROW + 1, :] * pitch)
    table = fetch_rows(items, plan, plan_sem)
    pieces = page // 2
    spacing = pieces + 1
    for c in range(pieces):
        spread[pl.ds(c, slots, stride=spacing), :] = lane_tile(rope_pages, c).astype(jnp.float32)
    for s in range(slots):
        for side in range(2):
            rows_of = spread[pl.ds(s * spacing + side, pieces // 2, stride=2), :]
            rope_keys[s, :, side * LANES : (side + 1) * LANES] = rows_of.astype(jnp.bfloat16)
    project_queries(message, w_uk, queries, heads, latent, narrow)
    score_work(queries, pool, rope_keys, scores, plan, None, table, 0, heads, scale)
    soften(scores, weights, norm, lse, rows * heads)


def own_values_kernel(
    items, pool, weights, norm, lse, w_uv, outs, logs, context, plan, plan_sem, *, heads
):
    rows = outs.shape[0]
    table = fetch_rows(items, plan, plan_sem)
    context[...] = jnp.zeros_like(context)
    logs[...] = heads_in_lanes(lse, rows, heads)
    value_work(pool, weights, context, plan, items, table, 0, heads, True)
    width = w_uv.shape[2]
    for h, out in head_outs(context, norm, w_uv, rows, heads):
        outs[:, h * width : (h + 1) * width] = out


def serve_kernel(
    message, pool, rope_keys, w_uk, w_uv, back,
    queries, scores, weights, norm, lse, context, items, plan, plan_sem,
    *, narrow, base,
):
    rows = message.shape[0]
    _, _, latent = pool.shape
    heads = w_uk.shape[0]
    scale = 1.0 / math.sqrt(w_uk.shape[1] + narrow // heads)
    asked = message[0:FIELDS, message.shape[1] - LANES :].astype(jnp.float32)
    items[...] = to_table(asked, asked[COUNT : COUNT + 1, :], rows, heads)
    table = fetch_rows(items, plan, plan_sem)
    project_queries(message, w_uk, queries, heads, latent, narrow)
    score_work(queries, pool, rope_keys, scores, plan, items, table, base, heads, scale)
    soften(scores, weights, norm, lse, rows * heads)
    value_work(pool, weights, context, plan, None, (), base, heads, False)
    width = w_uv.shape[2]
    lane = lax.broadcasted_iota(jnp.int32, (rows, LANES), 1)
    for h, out in head_outs(context, norm, w_uv, rows, heads):
        back[:, h * width : (h + 1) * width] = out.astype(jnp.bfloat16)
    logs = heads_in_lanes(lse, rows, heads)
    packed = jnp.zeros((rows, LANES), jnp.float32)
    for part in range(3):
        piece = logs.astype(jnp.bfloat16).astype(jnp.float32)
        logs = logs - piece
        packed = jnp.where(lane // heads == part, piece, packed)
    back[:, heads * width :] = packed.astype(jnp.bfloat16)


def join_kernel(outs, logs, from_a, from_b, w_o, sent, joined, *, heads):
    rows = outs.shape[0]
    width = outs.shape[1] // heads
    logs = [logs[...]]
    for arrived in (from_a, from_b):
        tile = arrived[:, heads * width :].astype(jnp.float32)
        logs.append(
            tile + pltpu.roll(tile, LANES - heads, 1) + pltpu.roll(tile, LANES - 2 * heads, 1)
        )
    peak = jnp.maximum(jnp.maximum(logs[0], logs[1]), logs[2])
    shares = [jnp.exp(one - peak) for one in logs]
    whole = 1.0 / (shares[0] + shares[1] + shares[2])
    shares = [share * whole for share in shares]
    for h in range(heads):
        at = slice(h * width, (h + 1) * width)
        top = 0.0
        for values, share in zip((outs, from_a, from_b), shares):
            mine = jnp.broadcast_to(share[:, h : h + 1], (rows, width))
            top = top + mine * values[:, at].astype(jnp.float32)
        joined[:, at] = top.astype(jnp.bfloat16)
    other = lax.rem(lax.axis_index("tp") + 1, lax.axis_size("tp"))
    project_out(joined, w_o, other, sent)


def project_out(joined, w_o, part, out):
    cols = out.shape[1]
    at = pl.ds(pl.multiple_of(part * cols, cols), cols)
    out[...] = jnp.dot(joined[...], w_o[:, at], preferred_element_type=jnp.float32).astype(out.dtype)


def keep_kernel(joined, w_o, kept):
    project_out(joined, w_o, lax.axis_index("tp"), kept)


def vmem():
    return pl.BlockSpec(memory_space=pltpu.VMEM)


def in_hbm(array):
    return pltpu.with_memory_space_constraint(array, pltpu.HBM)


def call(kernel, out, ins, scratch, limit, cost=None, **sizes):
    return pl.pallas_call(
        functools.partial(kernel, **sizes),
        out_shape=out,
        in_specs=ins,
        out_specs=jax.tree.map(lambda _: vmem(), out),
        scratch_shapes=scratch,
        compiler_params=pltpu.CompilerParams(vmem_limit_bytes=limit * MIB),
        cost_estimate=cost,
    )


def shards(
    q_nope, q_rope, lengths, page_table, lend_counts, latent_pages, rope_pages, w_uk, w_uv, w_o
):
    rows = lengths.shape[0]
    heads, nope, latent = w_uk.shape
    slots, page, _ = latent_pages.shape
    most = page_table.shape[1]
    width = w_uv.shape[2]
    narrow = q_rope.shape[1]
    tiles = latent // LANES
    units = most // LEND
    assert rows * units <= LANES and FIELDS <= rows <= LANES // 2 and page * LEND == LANES
    f32, bf16, i32 = jnp.float32, jnp.bfloat16, jnp.int32
    shape = jax.ShapeDtypeStruct
    sem = pltpu.SemaphoreType.DMA
    stats = (rows * heads, LANES)
    padded = (rows + 1) * heads
    pitched = -(-(rows + 1) * (heads + 1) // 8) * 8
    block = pltpu.VMEM((tiles + 2, pitched, LANES), f32)
    contexts = pltpu.VMEM((tiles, pitched, LANES), f32)
    plan = pltpu.SMEM((TABLE_ROWS * LANES,), i32)

    message, own = call(
        pack_kernel,
        (shape((rows, heads * nope + narrow + LANES), bf16), shape((FIELDS, LANES), i32)),
        [pl.BlockSpec(memory_space=pl.ANY)] * 5,
        [
            pltpu.VMEM((1, rows), i32),
            pltpu.VMEM((most, rows), i32),
            pltpu.VMEM((2, rows), i32),
            pltpu.VMEM((FIELDS, LANES), f32),
            sem((5,)),
        ],
        4,
        pl.CostEstimate(flops=20 * 10**9, bytes_accessed=64 * MIB, transcendentals=10**7),
        page=page,
    )(*map(in_hbm, (lengths.reshape(1, rows), page_table.T, lend_counts.T, q_nope, q_rope)))
    asked_b = swap(message, "dp", True)
    asked_a = swap(message, "dp", False)

    rope_keys, weights, norm, lse, items = call(
        own_scores_kernel,
        (
            shape((slots, page // 4, 2 * LANES), bf16),
            shape((units * padded, LANES), f32),
            shape(stats, f32),
            shape(stats, f32),
            shape((FIELDS, LANES), i32),
        ),
        [vmem()] * 5,
        [
            block,
            pltpu.VMEM((units * padded, LANES), f32),
            pltpu.VMEM((slots * (page // 2 + 1), LANES), f32),
            pltpu.VMEM((FIELDS, LANES), f32),
            plan,
            sem((TABLE_ROWS,)),
        ],
        24,
        pl.CostEstimate(
            flops=2 * rows * heads * most * page * (latent + LANES),
            bytes_accessed=slots * page * (latent + LANES) * 2,
            transcendentals=rows * heads * most * page,
        ),
        heads=heads,
        narrow=narrow,
        most=most,
    )(own, message, rope_pages, latent_pages, w_uk)

    serve_scratch = [
        block,
        pltpu.VMEM((padded, LANES), f32),
        pltpu.VMEM((padded, LANES), f32),
        pltpu.VMEM(stats, f32),
        pltpu.VMEM(stats, f32),
        contexts,
        pltpu.VMEM((FIELDS, LANES), i32),
        plan,
        sem((TABLE_ROWS,)),
    ]

    def serve(asked, base):
        return call(
            serve_kernel,
            shape((rows, heads * width + LANES), bf16),
            [vmem()] * 5,
            serve_scratch,
            8,
            narrow=narrow,
            base=base,
        )(asked, latent_pages, rope_keys, w_uk, w_uv)

    back_b = serve(asked_b, LANES // 2)
    from_b = swap(back_b, "dp", True)
    back_a = serve(asked_a, 0)
    from_a = swap(back_a, "dp", False)
    outs, logs = call(
        own_values_kernel,
        (shape((rows, heads * width), f32), shape((rows, LANES), f32)),
        [vmem()] * 6,
        [contexts, plan, sem((TABLE_ROWS,))],
        8,
        heads=heads,
    )(items, latent_pages, weights, norm, lse, w_uv)
    cols = w_o.shape[1] // lax.axis_size("tp")
    sent, joined = call(
        join_kernel,
        (shape((rows, cols), bf16), shape((rows, heads * width), bf16)),
        [vmem()] * 5,
        [],
        8,
        heads=heads,
    )(outs, logs, from_a, from_b, w_o)
    arrived = swap(sent, "tp", False)
    kept = call(keep_kernel, shape((rows, cols), f32), [vmem()] * 2, [], 8)(joined, w_o)
    return (kept + arrived.astype(f32)).astype(bf16)


def solution(mesh):
    in_specs = (
        P("dp", "tp"),
        P("dp", "tp"),
        P("dp"),
        P("dp", None),
        P("dp", None),
        P("dp", None, None),
        P("dp", None),
        P("tp", None, None),
        P("tp", None, None),
        P("tp", None),
    )
    out_specs = P("dp", "tp")

    return jax.shard_map(shards, mesh=mesh, in_specs=in_specs, out_specs=out_specs, check_vma=False)
```
